32 devices in a mesh: strike: 8 (over y, x, core), dip: 4 (over z).
Axes of the slice: x: 2, y: 2, z: 4, core: 2. Of those that a mesh axis runs over, the one named last changes fastest.
Arguments:
- slip: float32 [8192, 2048], P('strike', 'dip'), may hold values from -4 to 8
- slip_rate: float32 [8192, 2048], P('strike', 'dip'), may hold values from -6 to 6
- state: float32 [8192, 2048], P('strike', 'dip'), may hold values from -1 to 1
- loading: float32 [8192, 2048], P('strike', 'dip'), may hold values from -8 to 8
- normal_stress: float32 [8192, 2048], P('strike', 'dip'), may hold values from 0.5 to 2
- patch: int32 [8192, 2048], P('strike', 'dip'), may hold values from 0 to 3
- rate_coef: float32 [4], replicated, may hold values from 0.3 to 1
- state_coef: float32 [4], replicated, may hold values from 0.3 to 1
- slip_scale: float32 [4], replicated, may hold values from 0.5 to 2
- kernel: bfloat16 [16, 2048, 8192], P(None, ('strike', 'dip')), may hold values from -1.5 to 1.5
- history: bfloat16 [16, 2, 2048, 8192], P(None, None, ('strike', 'dip')), may hold values from -6 to 6
Outputs:
- new_rate: float32 [8192, 2048], P('strike', 'dip')
- new_state: float32 [8192, 2048], P('strike', 'dip')
- transfer_stress: float32 [8192, 2048], P('strike', 'dip')
- rate_modes: bfloat16 [2, 2048, 8192], P(None, ('strike', 'dip'))
The draws below stay inside these ranges and needn't reach their ends.
All inputs are finite; a program needn't handle non-finite values.
Results may differ from the reference program's by a relative error of at most 0.001.
Values sent between devices are 32-bit elements; how exact they have to be, the bound alone decides.
A program may use at most 192 MiB of HBM per device.

```python
import math
import jax
import jax.numpy as jnp

NX = 8192
NY = 2048
HIST = 16
PATCHES = 4
NEWTON = 8


def draw_slip(key, part):
    base = jax.random.fold_in(key, 4711)
    keys = jax.random.split(base, 6)
    along_x = jnp.arange(NX, dtype=jnp.float32)[:, None] / NX
    along_y = jnp.arange(NY, dtype=jnp.float32)[None, :] / NY
    wave_a = jax.random.randint(keys[0], (), 1, 4).astype(jnp.float32)
    wave_b = jax.random.randint(keys[1], (), 1, 3).astype(jnp.float32)
    phase_a = jax.random.uniform(keys[2], (), jnp.float32, 0.0, 2.0 * math.pi)
    phase_b = jax.random.uniform(keys[3], (), jnp.float32, 0.0, 2.0 * math.pi)
    rough = jnp.clip(jax.random.normal(keys[4], (NX, NY), jnp.float32), -4.0, 4.0)
    level = jax.random.uniform(keys[5], (), jnp.float32, 1.5, 2.5)
    amp_a = 0.8
    amp_b = 0.5
    smooth = level + amp_a * jnp.cos(2.0 * math.pi * wave_a * along_x + phase_a) + amp_b * jnp.cos(2.0 * math.pi * wave_b * along_y + phase_b)
    return (rough + smooth).astype(jnp.float32)


def with_ends(values, rng, low, high):
    index_at = [jax.random.randint(jax.random.fold_in(rng, axis), (), 0, length) for axis, length in enumerate(values.shape)]
    longest = values.shape.index(max(values.shape))
    beside = index_at[:longest] + [(index_at[longest] + 1) % values.shape[longest]] + index_at[longest + 1:]
    return values.at[tuple(index_at)].set(low).at[tuple(beside)].set(high)


def steps_of(key, shape, cuts, low, largest):
    loudness = 1.0
    for dim, parts in cuts:
        steps = jax.random.uniform(jax.random.fold_in(jax.random.fold_in(key, 6), dim), (parts,), jnp.float32, low / len(cuts), largest / len(cuts))
        loudness = loudness * jnp.repeat(jnp.exp(steps), shape[dim] // parts).reshape((-1,) + (1,) * (len(shape) - 1 - dim))
    return loudness


def bell_draw(key, extent, width, most, cuts=(), kind=jnp.bfloat16):
    entries = width * jax.random.normal(key, extent, jnp.float32)
    if cuts:
        entries = entries * steps_of(key, extent, cuts, -0.22, 0.18)
    return jnp.clip(entries, -most, most).astype(kind)


def setup_inputs(seed: int = 0) -> dict:
    splits = jax.random.split(jax.random.key(seed), 12)
    return {
        "slip": draw_slip(jax.random.fold_in(splits[11], 71), 0),
        "slip_rate": bell_draw(splits[1], (NX, NY), 1.0, 6.0, ((0, 8), (1, 4)), jnp.float32),
        "state": jnp.clip(jax.random.uniform(splits[2], (NX, NY), jnp.float32, -1.0, 1.0) * steps_of(splits[2], (NX, NY), ((0, 8), (1, 4)), -0.4, 0.0), -1.0, 1.0),
        "loading": bell_draw(splits[3], (NX, NY), 2.0, 8.0, ((0, 8), (1, 4)), jnp.float32),
        "normal_stress": jnp.clip(jnp.exp(math.log(2.0) - 1.3862944 * jax.random.uniform(splits[4], (NX, NY), jnp.float32) ** steps_of(splits[4], (NX, NY), ((0, 8), (1, 4)), -0.2, 0.2)), 0.5, 2.0),
        "patch": with_ends(jax.random.randint(splits[5], (NX, NY), 0, PATCHES), jax.random.fold_in(splits[5], 1), 0, PATCHES - 1).astype(jnp.int32),
        "rate_coef": jnp.clip(jnp.exp(jax.random.uniform(splits[6], (PATCHES,), jnp.float32, math.log(0.3), math.log(1.0))), 0.3, 1.0),
        "state_coef": jnp.clip(jnp.exp(jax.random.uniform(splits[7], (PATCHES,), jnp.float32, math.log(0.3), math.log(1.0))), 0.3, 1.0),
        "slip_scale": jnp.clip(jnp.exp(jax.random.uniform(splits[8], (PATCHES,), jnp.float32, math.log(0.5), math.log(2.0))), 0.5, 2.0),
        "kernel": bell_draw(splits[9], (HIST, NY, NX), HIST ** -0.5, 1.5, ((1, 32),)),
        "history": bell_draw(splits[10], (HIST, 2, NY, NX), 1.0, 6.0, ((2, 32),)),
    }


shear_modulus = 1.0
damping = 0.5
relaxation = 0.35
time_step = 0.1

def inverse_sinh(value):
    size_v = jnp.abs(value)
    square = size_v * size_v
    result = jnp.log1p(size_v + square / (1.0 + jnp.sqrt(square + 1.0)))
    return jnp.where(value < 0.0, -result, result)

def lookup(patch, table):
    result = jnp.zeros(patch.shape, jnp.float32)
    for label in range(PATCHES):
        result = jnp.where(patch == label, table[label], result)
    return result

def friction(slip_rate, state, loading, normal_stress, transfer, coef_a, coef_b, length_l):
    stress = loading + transfer
    prefix = 2.0 * jnp.exp(-state / coef_a)
    angle_w = inverse_sinh(slip_rate / prefix)
    for iteration in range(NEWTON):
        residue = normal_stress * coef_a * angle_w + damping * prefix * jnp.sinh(angle_w) - stress
        slope = normal_stress * coef_a + damping * prefix * jnp.cosh(angle_w)
        ratio = residue / slope
        angle_w = angle_w - relaxation * ratio / (1.0 + jnp.abs(ratio))
    new_rate = prefix * jnp.sinh(angle_w)
    new_state = state + time_step * (coef_b / length_l) * (jnp.exp(-state / coef_b) - jnp.abs(new_rate))
    return (new_rate, new_state)

def wavenumber(count):
    index = jnp.arange(count, dtype=jnp.int32)
    return 2.0 * math.pi / count * ((index + count // 2) % count - count // 2).astype(jnp.float32)

def reference(slip, slip_rate, state, loading, normal_stress, patch, rate_coef, state_coef, slip_scale, kernel, history):
    slip_hat = jnp.fft.fft2(slip, norm='ortho').T
    rate_hat = jnp.fft.fft2(slip_rate, norm='ortho').T
    wave_x = wavenumber(NX)
    wave_y = wavenumber(NY)
    magnitude = jnp.sqrt(wave_y[:, None] ** 2 + wave_x[None, :] ** 2)
    kernel_full = kernel.astype(jnp.float32)
    memory_re = jnp.einsum('jrc,jrc->rc', kernel_full, history[:, 0].astype(jnp.float32))
    memory_im = jnp.einsum('jrc,jrc->rc', kernel_full, history[:, 1].astype(jnp.float32))
    static = -0.5 * shear_modulus * magnitude
    stress_re = static * jnp.real(slip_hat).astype(jnp.float32) + memory_re
    stress_im = static * jnp.imag(slip_hat).astype(jnp.float32) + memory_im
    stress_hat = (stress_re + 1j * stress_im).T
    transfer = jnp.real(jnp.fft.ifft2(stress_hat, norm='ortho')).astype(jnp.float32)
    rate_modes = jnp.stack([jnp.real(rate_hat), jnp.imag(rate_hat)]).astype(jnp.bfloat16)
    coef_a = lookup(patch, rate_coef)
    coef_b = lookup(patch, state_coef)
    length_l = lookup(patch, slip_scale)
    new_rate, new_state = friction(slip_rate, state, loading, normal_stress, transfer, coef_a, coef_b, length_l)
    return (new_rate, new_state, transfer, rate_modes)
```

```python
import functools
import math

import jax
import jax.numpy as jnp
import numpy as np
from jax import lax
from jax.experimental import pallas as pl
from jax.experimental.pallas import tpu as pltpu
from jax.sharding import PartitionSpec as P

NEWTON = 8


shear_modulus = 1.0
damping = 0.5
relaxation = 0.35
time_step = 0.1


def inverse_sinh(value):
    size_v = jnp.abs(value)
    square = size_v * size_v
    result = jnp.log1p(size_v + square / (1.0 + jnp.sqrt(square + 1.0)))
    return jnp.where(value < 0.0, -result, result)


def exact_tables(rows, cols, modulus, sign):
    angles = 2.0 * math.pi / modulus * (rows * cols % modulus).astype(jnp.float32)
    return (jnp.cos(angles), sign * jnp.sin(angles))


def grid_tables(count_in, count_out, modulus, sign):
    row_index = lax.broadcasted_iota(jnp.int32, (count_in, count_out), 0)
    col_index = lax.broadcasted_iota(jnp.int32, (count_in, count_out), 1)
    return exact_tables(row_index, col_index, modulus, sign)


def complex_table(count, sign, scale=1.0):
    cos, sin = grid_tables(count, count, count, sign)
    cos, sin = cos * scale, sin * scale
    return jnp.stack([jnp.stack([cos, sin], 1), jnp.stack([-sin, cos], 1)], 0)


def product(pattern, left_op, right_op):
    return jnp.einsum(pattern, left_op, right_op, precision=lax.Precision.HIGH)


def twist(part_re, part_im, table_re, table_im):
    return (
        part_re * table_re - part_im * table_im,
        part_re * table_im + part_im * table_re,
    )


INNER = 128


def wavenumber(index, count):
    return 2.0 * math.pi / count * ((index + count // 2) % count - count // 2).astype(jnp.float32)


def friction_kernel(
    labels,
    filled,
    rate_coef,
    state_coef,
    slip_scale,
    transfer_in,
    slip_rate_in,
    state_in,
    loading_in,
    normal_in,
    patch_in,
    *refs,
):
    new_rate_out, new_state_out, transfer_out = refs[filled:]
    patch = patch_in[...]

    def choose(table):
        result = jnp.zeros(patch.shape, jnp.float32)
        for label in range(labels):
            result = jnp.where(patch == label, table[label], result)
        return result

    coef_a = choose(rate_coef)
    coef_b = choose(state_coef)
    length_l = choose(slip_scale)
    transfer = transfer_in[0, 0] + transfer_in[1, 0]
    state = state_in[...]
    stress = loading_in[...] + transfer
    prefix = 2.0 * jnp.exp(-state / coef_a)
    angle_w = inverse_sinh(slip_rate_in[...] / prefix)
    weight = normal_in[...] * coef_a
    half = 0.5 * damping * prefix
    for iteration in range(NEWTON):
        grow = half * jnp.exp(angle_w)
        decay = half * jnp.exp(-angle_w)
        residue = weight * angle_w + (grow - decay) - stress
        slope = weight + (grow + decay)
        angle_w = angle_w - relaxation * residue / (slope + jnp.abs(residue))
    new_rate = (0.5 * prefix) * (jnp.exp(angle_w) - jnp.exp(-angle_w))
    new_rate_out[...] = new_rate
    new_state_out[...] = state + time_step * (coef_b / length_l) * (
        jnp.exp(-state / coef_b) - jnp.abs(new_rate)
    )
    transfer_out[...] = transfer


def friction(part, parts, tables, transfer, cells, before):
    _, sources, rows, columns = transfer.shape
    block = pl.BlockSpec((rows, columns), lambda step: (step * parts + part, 0))
    scalar = pl.BlockSpec(memory_space=pltpu.SMEM)
    size = transfer.size // 2
    first = len(tables) + 1 + len(cells)
    return pl.pallas_call(
        functools.partial(friction_kernel, tables[0].shape[0], len(before)),
        grid=(sources,),
        out_shape=[jax.ShapeDtypeStruct(cells[0].shape, jnp.float32)] * 3,
        in_specs=[scalar] * len(tables)
        + [pl.BlockSpec((2, 1, rows, columns), lambda step: (0, step, 0, 0))]
        + [block] * len(cells)
        + [pl.BlockSpec(memory_space=pl.ANY)] * len(before),
        out_specs=[block] * 3,
        input_output_aliases={first + index: index for index in range(len(before))},
        compiler_params=pltpu.CompilerParams(vmem_limit_bytes=32 * 1024 * 1024),
        cost_estimate=pl.CostEstimate(
            flops=size * 200, bytes_accessed=size * 36, transcendentals=size * 30
        ),
    )(*tables, transfer, *cells, *before)


def band_rows(part_re, part_im, sign):
    rows, total = part_re.shape
    outer = total // INNER
    table = complex_table(outer, sign).reshape(2 * outer, 2, outer)
    both = jnp.concatenate(
        [part_re.reshape(rows, outer, INNER), part_im.reshape(rows, outer, INNER)], 1
    )
    first = product("rab,akc->krcb", both, table)
    twist_re, twist_im = grid_tables(outer, INNER, total, sign)
    first = jnp.concatenate(twist(first[0], first[1], twist_re, twist_im), -1)
    second = complex_table(INNER, sign, 1.0 / math.sqrt(total)).reshape(2 * INNER, 2, INNER)
    return [
        product("rcb,bm->rmc", first, second[:, part]).reshape(rows, total) for part in range(2)
    ]


def dip_table(strike_count, dip_count, band, total):
    half = dip_count // 2
    index = np.arange(total).reshape(strike_count, 2, half, band).transpose(1, 0, 2, 3)
    turn = index[..., None] * np.arange(total) % total * (2.0 * np.pi / total)
    table = np.stack([np.cos(turn), -np.sin(turn)], 3) / math.sqrt(total)
    return table.astype(np.float32)


def per_device(
    slip,
    slip_rate,
    state,
    loading,
    normal_stress,
    patch,
    rate_coef,
    state_coef,
    slip_scale,
    kernel,
    history,
):
    strike_count = lax.axis_size("strike")
    dip_count = lax.axis_size("dip")
    half = dip_count // 2
    both_axes = ("strike", "dip")
    cells_x, cells_y = slip.shape
    band, total_x = kernel.shape[1:]
    total_y = cells_y * dip_count
    rows = cells_x // half
    strike, dip = lax.axis_index("strike"), lax.axis_index("dip")
    side, place = dip // half, dip % half
    sides = [
        [s * dip_count + t * half + k for s in range(strike_count) for k in range(half)]
        for t in range(2)
    ]

    def after(value, earlier):
        return lax.optimization_barrier((value, earlier))

    def across_half(array):
        return lax.all_to_all(
            array, both_axes, split_axis=0, concat_axis=0, tiled=True, axis_index_groups=sides
        )

    tables = jnp.asarray(dip_table(strike_count, dip_count, band, total_y))
    table = lax.dynamic_index_in_dim(tables, side, 0, keepdims=False)

    slip_half = jnp.zeros((cells_x, half * cells_y), jnp.float32)
    slip_half = lax.dynamic_update_slice(slip_half, slip, (0, place * cells_y))
    for turn in range(1, half):
        moved = lax.ppermute(
            slip,
            "dip",
            [
                (d, d // half * half + (d + turn) % half)
                for d in range(dip_count)
            ],
        )
        slip_half = lax.dynamic_update_slice(
            slip_half, moved, (0, (place + half - turn) % half * cells_y)
        )
    columns = lax.dynamic_slice_in_dim(table, side * half * cells_y, half * cells_y, 4)
    mine = lax.dynamic_index_in_dim(columns, place, 1, keepdims=False)
    slip_modes = product("zkrj,ij->zkri", mine, slip_half)
    other = lax.dynamic_index_in_dim(tables, 1 - side, 0, keepdims=False)[:, 0, :, 0]
    other = lax.dynamic_slice_in_dim(other, side * half * cells_y, half * cells_y, 2)
    extra = product("zkj,ij->zki", other, slip_half)
    extra = lax.ppermute(extra, "dip", [(0, half), (half, 0)])
    slip_modes = slip_modes.at[:, :, 0].add(extra)

    slip_both = lax.all_to_all(slip_modes, "strike", split_axis=0, concat_axis=0, tiled=True)
    slip_both = slip_both.transpose(1, 2, 0, 3).reshape(2, band, total_x)

    rate_rows = jnp.zeros((rows, total_y), jnp.float32)
    for turn in range(dip_count):
        share = lax.dynamic_slice_in_dim(slip_rate, (dip + turn) % half * rows, rows, 0)
        if turn:
            share = lax.ppermute(
                share, "dip", [(d, (d + turn) % dip_count) for d in range(dip_count)]
            )
        rate_rows = lax.dynamic_update_slice(
            rate_rows, share, (0, (dip + dip_count - turn) % dip_count * cells_y)
        )
    rate_parts = product("zpkrj,ij->zpkri", table, rate_rows)
    rate_parts = rate_parts.reshape(strike_count * half, 2, band, rows)

    slip_re, slip_im = band_rows(slip_both[0], slip_both[1], -1.0)
    offset = (strike * dip_count + dip) * band
    row_index = lax.broadcasted_iota(jnp.int32, (band,), 0)
    wave_y = wavenumber(offset + row_index, total_y)
    wave_x = wavenumber(lax.broadcasted_iota(jnp.int32, (total_x,), 0), total_x)
    magnitude = jnp.sqrt(wave_y[:, None] ** 2 + wave_x[None, :] ** 2)
    times = jnp.where((row_index == 0) & (place == 0), 1.0, 2.0)
    static = -0.5 * shear_modulus * magnitude * times[:, None]
    memory_re = jnp.einsum("jrc,jrc->rc", kernel, history[:, 0], preferred_element_type=jnp.float32)
    memory_im = jnp.einsum("jrc,jrc->rc", kernel, history[:, 1], preferred_element_type=jnp.float32)
    stress_re = static * slip_re + memory_re
    stress_im = static * slip_im + memory_im
    back_parts = band_rows(stress_re, stress_im, 1.0)

    back = jnp.stack(back_parts).reshape(2, band, strike_count * half, rows).transpose(2, 0, 1, 3)
    back, rate_parts = after(back, rate_parts)
    back = across_half(back)
    rate_parts, back = after(rate_parts, back)
    rate_both = across_half(rate_parts)

    flat = table.reshape(strike_count * half * 2 * band, total_y)
    line = product("mi,mj->ij", back.reshape(-1, rows), flat)
    line = line.reshape(rows, dip_count, cells_y).transpose(1, 0, 2)
    parts = 2
    step = rows // parts
    cells = (slip_rate, state, loading, normal_stress, patch)
    pieces = []
    for part in range(parts):
        piece = line[:, part * step : (part + 1) * step]
        piece = lax.all_to_all(piece, "dip", split_axis=0, concat_axis=0, tiled=True)
        pieces.append(piece.reshape(2, half, step, cells_y))
    rate_both = rate_both.transpose(1, 2, 0, 3).reshape(2, band, total_x)
    rate_modes = jnp.stack(band_rows(rate_both[0], rate_both[1], -1.0)).astype(jnp.bfloat16)
    outs = []
    for part in range(parts):
        outs = friction(
            part, parts, (rate_coef, state_coef, slip_scale), pieces[part], cells, outs
        )
    return (*outs, rate_modes)


def solution(mesh):
    return jax.shard_map(
        per_device,
        mesh=mesh,
        in_specs=(
            P("strike", "dip"),
            P("strike", "dip"),
            P("strike", "dip"),
            P("strike", "dip"),
            P("strike", "dip"),
            P("strike", "dip"),
            P(),
            P(),
            P(),
            P(None, ("strike", "dip"), None),
            P(None, None, ("strike", "dip"), None),
        ),
        out_specs=(
            P("strike", "dip"),
            P("strike", "dip"),
            P("strike", "dip"),
            P(None, ("strike", "dip"), None),
        ),
        check_vma=False,
    )
```

```python
import functools
import math

import jax
import jax.numpy as jnp
import numpy as np
from jax import lax
from jax.experimental import pallas as pl
from jax.experimental.pallas import tpu as pltpu
from jax.sharding import PartitionSpec as P

NEWTON = 8


shear_modulus = 1.0
damping = 0.5
relaxation = 0.35
time_step = 0.1


def inverse_sinh(value):
    size_v = jnp.abs(value)
    square = size_v * size_v
    result = jnp.log1p(size_v + square / (1.0 + jnp.sqrt(square + 1.0)))
    return jnp.where(value < 0.0, -result, result)


INNER = 128
SUB = 8
CHUNKS = 4
MESH = pl.DeviceIdType.MESH


def wavenumber(index, count):
    return 2.0 * math.pi / count * ((index + count // 2) % count - count // 2).astype(jnp.float32)


def friction_kernel(
    labels,
    filled,
    where_in,
    rate_coef,
    state_coef,
    slip_scale,
    transfer_in,
    transfer_add,
    slip_rate_in,
    state_in,
    loading_in,
    normal_in,
    patch_in,
    *refs,
):
    new_rate_out, new_state_out, transfer_out = refs[filled:]
    patch = patch_in[...]

    def choose(table):
        result = jnp.zeros(patch.shape, jnp.float32)
        for label in range(labels):
            result = jnp.where(patch == label, table[label], result)
        return result

    coef_a = choose(rate_coef)
    coef_b = choose(state_coef)
    length_l = choose(slip_scale)
    transfer = transfer_in[...] + transfer_add[...]
    state = state_in[...]
    stress = loading_in[...] + transfer
    prefix = 2.0 * jnp.exp(-state / coef_a)
    angle_w = inverse_sinh(slip_rate_in[...] / prefix)
    weight = normal_in[...] * coef_a
    half = 0.5 * damping * prefix
    for iteration in range(NEWTON):
        grow = half * jnp.exp(angle_w)
        decay = half * jnp.exp(-angle_w)
        residue = weight * angle_w + (grow - decay) - stress
        slope = weight + (grow + decay)
        angle_w = angle_w - relaxation * residue / (slope + jnp.abs(residue))
    new_rate = (0.5 * prefix) * (jnp.exp(angle_w) - jnp.exp(-angle_w))
    new_rate_out[...] = new_rate
    new_state_out[...] = state + time_step * (coef_b / length_l) * (
        jnp.exp(-state / coef_b) - jnp.abs(new_rate)
    )
    transfer_out[...] = transfer


def friction(where, tables, transfers, cells, earlier, before):
    rows, columns = transfers[0].shape
    blocks = 2
    step_rows = rows // blocks
    block = pl.BlockSpec((step_rows, columns), lambda step, where: (where[0] * blocks + step, 0))
    local = pl.BlockSpec((step_rows, columns), lambda step, where: (step, 0))
    scalar = pl.BlockSpec(memory_space=pltpu.SMEM)
    size = rows * columns
    first = 1 + len(tables) + 2 + len(cells) + len(earlier)
    kept = len(earlier) + len(before)
    return pl.pallas_call(
        functools.partial(friction_kernel, tables[0].shape[0], kept),
        out_shape=[jax.ShapeDtypeStruct(cells[0].shape, jnp.float32)] * 3,
        grid_spec=pltpu.PrefetchScalarGridSpec(
            num_scalar_prefetch=1,
            grid=(blocks,),
            in_specs=[scalar] * len(tables)
            + [local] * 2
            + [block] * len(cells)
            + [pl.BlockSpec(memory_space=pl.ANY)] * kept,
            out_specs=[block] * 3,
        ),
        input_output_aliases={first + index: index for index in range(len(before))},
        compiler_params=pltpu.CompilerParams(vmem_limit_bytes=32 * 1024 * 1024),
        cost_estimate=pl.CostEstimate(
            flops=size * 200, bytes_accessed=size * 40, transcendentals=size * 30
        ),
    )(where, *tables, *transfers, *cells, *earlier, *before)


def split_parts(value):
    high = value.astype(jnp.bfloat16)
    return np.stack([high, (value - high.astype(np.float32)).astype(jnp.bfloat16)])


def dip_tables(strike_count, dip_count, band, total):
    half = dip_count // 2
    index = np.arange(total).reshape(strike_count, 2, half, band).transpose(1, 2, 0, 3)
    turn = index[..., None] * np.arange(total) % total * (2.0 * np.pi / total)
    table = np.stack([np.cos(turn), -np.sin(turn)], 3) / math.sqrt(total)
    mirrored = table[:, 0, :, :, 0].reshape(2, strike_count * 2, total)
    table = table.reshape(2, half, strike_count * 2 * band, total)
    return [
        np.ascontiguousarray(np.moveaxis(split_parts(part.astype(np.float32)), 0, 1))
        for part in (table, mirrored)
    ]


def lane_order(outer):
    fold = INNER // outer
    return (np.arange(outer)[None, :] * fold + np.arange(fold)[:, None]).reshape(-1)


def strike_tables(total, sources):
    outer = total // INNER
    order = lane_order(outer)
    turn = np.arange(INNER)[:, None] * order[None, :] % INNER * (2.0 * np.pi / INNER)
    cos, sin = np.cos(turn) / math.sqrt(total), np.sin(turn) / math.sqrt(total)
    there = np.block([[cos, -sin], [sin, cos]])
    back = np.block([[cos.T, sin.T], [-sin.T, cos.T]])
    both = np.stack([there, back]).astype(np.float32)
    high = both.astype(jnp.bfloat16)
    low = (both - high.astype(np.float32)).astype(jnp.bfloat16)
    twist = np.arange(outer)[:, None] * np.arange(INNER)[None, :] * (2.0 * np.pi / total)
    twist = np.stack([np.cos(twist), np.sin(twist)])
    tiles = outer // sources
    small = np.arange(sources)[:, None] * np.arange(tiles)[None, :] * (2.0 * np.pi / outer)
    small = np.stack([np.cos(small), np.sin(small)]).reshape(2, outer)
    twists = np.stack([twist, np.broadcast_to(small[:, :, None], twist.shape)])
    twists = np.broadcast_to(twists[:, :, :, None, :], (2, 2, outer, SUB, INNER))
    return np.stack([high, low], 1), np.ascontiguousarray(twists.astype(np.float32))


def times_root(value, step, count, sign):
    re, im = value
    if step == 0:
        return re, im
    if 4 * step == count:
        return (-im, re) if sign > 0 else (im, -re)
    if 8 * step == count or 8 * step == 3 * count:
        root = math.sqrt(0.5)
        if sign > 0:
            turned = (re - im, re + im) if 8 * step == count else (-re - im, re - im)
        else:
            turned = (re + im, im - re) if 8 * step == count else (im - re, -re - im)
        return turned[0] * root, turned[1] * root
    cos = math.cos(2.0 * math.pi * step / count)
    sin = sign * math.sin(2.0 * math.pi * step / count)
    return re * cos - im * sin, re * sin + im * cos


def short_transform(values, sign):
    count = len(values)
    if count == 1:
        return values
    even = short_transform(values[0::2], sign)
    odd = short_transform(values[1::2], sign)
    low, high = [], []
    for step in range(count // 2):
        turned = times_root(odd[step], step, count, sign)
        low.append((even[step][0] + turned[0], even[step][1] + turned[1]))
        high.append((even[step][0] - turned[0], even[step][1] - turned[1]))
    return low + high


def exact_dot(left, table):
    high = left.astype(jnp.bfloat16)
    low = (left - high.astype(jnp.float32)).astype(jnp.bfloat16)
    dot = functools.partial(jnp.dot, preferred_element_type=jnp.float32)
    return dot(high, table[0]) + (dot(low, table[0]) + dot(high, table[1]))


def forward(load, turns_in, twists_in, spectrum, grid, sources):
    outer = twists_in.shape[2]
    tiles = outer // sources
    values = [(load(source, 0), load(source, 1)) for source in range(sources)]
    for at, (re, im) in enumerate(short_transform(values, -1.0)):
        lines = slice(at * tiles, (at + 1) * tiles)
        cos, sin = twists_in[1, 0, lines], twists_in[1, 1, lines]
        grid[0, at] = re * cos + im * sin
        grid[1, at] = im * cos - re * sin
    values = [(grid[0, :, tile], grid[1, :, tile]) for tile in range(tiles)]
    for at, (re, im) in enumerate(short_transform(values, -1.0)):
        lines = slice(at * sources, (at + 1) * sources)
        cos, sin = twists_in[0, 0, lines], twists_in[0, 1, lines]
        lines = slice(at * sources * SUB, (at + 1) * sources * SUB)
        spectrum[lines, :INNER] = (re * cos + im * sin).reshape(-1, INNER)
        spectrum[lines, INNER:] = (im * cos - re * sin).reshape(-1, INNER)
    spectrum[...] = exact_dot(spectrum[...], turns_in[0])


def backward(store, turns_in, twists_in, spectrum, grid, sources):
    outer = twists_in.shape[2]
    tiles = outer // sources
    spectrum[...] = exact_dot(spectrum[...], turns_in[1])
    values = []
    for at in range(tiles):
        lines = slice(at * sources * SUB, (at + 1) * sources * SUB)
        re = spectrum[lines, :INNER].reshape(sources, SUB, INNER)
        im = spectrum[lines, INNER:].reshape(sources, SUB, INNER)
        lines = slice(at * sources, (at + 1) * sources)
        cos, sin = twists_in[0, 0, lines], twists_in[0, 1, lines]
        values.append((re * cos - im * sin, re * sin + im * cos))
    for tile, (re, im) in enumerate(short_transform(values, 1.0)):
        grid[0, :, tile] = re
        grid[1, :, tile] = im
    values = []
    for at in range(sources):
        lines = slice(at * tiles, (at + 1) * tiles)
        cos, sin = twists_in[1, 0, lines], twists_in[1, 1, lines]
        re, im = grid[0, at], grid[1, at]
        values.append((re * cos - im * sin, re * sin + im * cos))
    for source, pair in enumerate(short_transform(values, 1.0)):
        for part in range(2):
            store(source, part, pair[part])


def reorder(source, target, outer):
    lane = lax.broadcasted_iota(jnp.int32, (outer, INNER), 1)
    for row in range(0, SUB, 2):
        pair = [source[pl.ds(row + at, outer, stride=SUB), :] for at in range(2)]
        turned = jnp.concatenate(pair, 0).T
        upper, lower = turned[:outer], turned[outer:]
        first = jnp.where(lane < outer, upper, pltpu.roll(lower, outer, 1))
        second = jnp.where(lane < outer, pltpu.roll(upper, outer, 1), lower)
        target[pl.ds(row, outer, stride=SUB), :] = first
        target[pl.ds(row + 1, outer, stride=SUB), :] = second


def dot_rows(table, value):
    high = value.astype(jnp.bfloat16)
    low = (value - high.astype(jnp.float32)).astype(jnp.bfloat16)

    def dot(left, right):
        return lax.dot_general(
            left, right, (((1,), (1,)), ((), ())), preferred_element_type=jnp.float32
        )

    return dot(table[0], high) + (dot(table[0], low) + dot(table[1], high))


def stress_kernel(
    strike_count,
    dip_count,
    slip,
    rate,
    kernel,
    history,
    table_all,
    mirror_all,
    turns_in,
    twists_in,
    back_out,
    rate_out,
    slip_held,
    made,
    held,
    sent,
    table,
    mirror,
    extra_made,
    extra_held,
    kernel_held,
    history_held,
    memory,
    spectrum,
    grid,
    natural,
    mixed,
    rate_held,
    joined,
    table_held,
    rate_made,
    local_sem,
    table_sem,
    rate_out_sem,
    memory_sem,
    slip_sem,
    extra_sem,
    band_sem,
    own_sem,
    rate_sem,
    back_sem,
    back_own_sem,
):
    half = dip_count // 2
    strike, dip = lax.axis_index("strike"), lax.axis_index("dip")
    side, place = dip // half, dip % half
    cells_x, cells_y = slip.shape
    lags, _, band, total_x = history.shape
    total_y = cells_y * dip_count
    rows = cells_x // half
    group = strike_count * half
    me = strike * half + place
    chunk = cells_x // CHUNKS
    outer = total_x // INNER
    tiles = outer // strike_count

    def in_half(index):
        return (index // half, side * half + index % half)

    barrier = pltpu.get_barrier_semaphore()

    @pl.loop(1, group)
    def _(offset):
        pl.semaphore_signal(
            barrier, inc=1, device_id=in_half((me + offset) % group), device_id_type=MESH
        )

    for other in range(half):
        pl.semaphore_signal(
            barrier,
            inc=1,
            device_id=(strike, (1 - side) * half + other),
            device_id_type=MESH,
        )
    pl.semaphore_wait(barrier, group - 1 + half)

    def slip_copy(offset, part):
        lines = pl.ds(part * chunk, chunk)
        return pltpu.make_async_remote_copy(
            src_ref=slip.at[lines],
            dst_ref=slip_held.at[place, lines],
            send_sem=slip_sem.at[0, offset - 1, part],
            recv_sem=slip_sem.at[1, offset - 1, part],
            device_id=(strike, side * half + (place + offset) % half),
            device_id_type=MESH,
        )

    for part in range(CHUNKS):
        for offset in range(1, half):
            slip_copy(offset, part).start()
    columns = pl.ds(pl.multiple_of(side * half * cells_y, INNER), half * cells_y)
    firsts = [
        pltpu.make_async_copy(slip, slip_held.at[place], local_sem.at[0]),
        pltpu.make_async_copy(table_all.at[side, :, place, :, columns], table, local_sem.at[1]),
        pltpu.make_async_copy(mirror_all.at[1 - side, :, :, columns], mirror, local_sem.at[2]),
        pltpu.make_async_copy(
            rate.at[pl.ds(pl.multiple_of(place * rows, SUB), rows)], rate_held.at[0], local_sem.at[3]
        ),
    ]
    for copy in firsts:
        copy.start()

    depth, width = kernel_held.shape[2:]
    across = total_x // width
    steps = band // depth * across

    def memory_copies(step, slot):
        lines = pl.ds(pl.multiple_of(step // across * depth, depth), depth)
        lanes = pl.ds(pl.multiple_of(step % across * width, width), width)
        return (
            pltpu.make_async_copy(
                kernel.at[:, lines, lanes], kernel_held.at[slot], memory_sem.at[0, slot]
            ),
            pltpu.make_async_copy(
                history.at[:, :, lines, lanes], history_held.at[slot], memory_sem.at[1, slot]
            ),
        )

    for copy in memory_copies(0, 0):
        copy.start()

    def memory_step(step):
        slot = step % 2

        @pl.when(step + 1 < steps)
        def _():
            for copy in memory_copies(step + 1, 1 - slot):
                copy.start()

        for copy in memory_copies(step, slot):
            copy.wait()
        piece = 2 * INNER

        @pl.loop(0, width // piece)
        def _(at):
            lanes = pl.ds(pl.multiple_of(at * piece, piece), piece)
            sums = [jnp.zeros((depth, piece), jnp.float32) for _ in range(2)]
            for lag in range(lags):
                factor = kernel_held[slot, lag, :, lanes].astype(jnp.float32)
                for part in range(2):
                    past = history_held[slot, lag, part, :, lanes].astype(jnp.float32)
                    sums[part] = sums[part] + factor * past
            lines = pl.ds(pl.multiple_of(step // across * depth, depth), depth)
            lanes = pl.ds(pl.multiple_of(step % across * width + at * piece, piece), piece)
            for part in range(2):
                memory[part, lines, lanes] = sums[part]

    def rate_copy(turn):
        target = (dip + turn) % dip_count
        lines = pl.ds(pl.multiple_of(target % half * rows, SUB), rows)
        return pltpu.make_async_remote_copy(
            src_ref=rate.at[lines],
            dst_ref=rate_held.at[turn],
            send_sem=rate_sem.at[0, turn - 1],
            recv_sem=rate_sem.at[1, turn - 1],
            device_id=(strike, target),
            device_id_type=MESH,
        )

    def extra_copy(part):
        lanes = pl.ds(pl.multiple_of(part * chunk, INNER), chunk)
        return pltpu.make_async_remote_copy(
            src_ref=extra_made.at[:, lanes],
            dst_ref=extra_held.at[:, lanes],
            send_sem=extra_sem.at[0, part],
            recv_sem=extra_sem.at[1, part],
            device_id=(strike, (dip + half) % dip_count),
            device_id_type=MESH,
        )

    def band_copy(offset, part):
        lanes = pl.ds(pl.multiple_of(part * chunk, INNER), chunk)
        target = (strike + offset) % strike_count
        return pltpu.make_async_remote_copy(
            src_ref=made.at[target, :, :, lanes],
            dst_ref=held.at[strike, :, :, lanes],
            send_sem=band_sem.at[0, offset - 1, part],
            recv_sem=band_sem.at[1, offset - 1, part],
            device_id=(target, dip),
            device_id_type=MESH,
        )

    def own_copy(part):
        lanes = pl.ds(pl.multiple_of(part * chunk, INNER), chunk)
        return pltpu.make_async_copy(
            made.at[strike, :, :, lanes], held.at[strike, :, :, lanes], own_sem.at[part]
        )

    def start_rate(turn, early):
        middle = ((dip == half - 1) & (turn == 1)) | ((dip == half) & (turn == dip_count - 1))

        @pl.when(middle == early)
        def _():
            rate_copy(turn).start()

    for turn in range(1, dip_count):
        start_rate(turn, True)
    for copy in firsts:
        copy.wait()

    @pl.loop(0, CHUNKS)
    def _(part):
        for offset in range(1, half):
            slip_copy(offset, part).wait()

        @pl.when(part == CHUNKS - 1)
        def _():
            for turn in range(1, dip_count):
                start_rate(turn, False)

        lines = pl.ds(pl.multiple_of(part * chunk, SUB), chunk)
        lanes = pl.ds(pl.multiple_of(part * chunk, INNER), chunk)
        blocks = [slip_held[block, lines] for block in range(half)]
        extra = sum(
            dot_rows(mirror[:, :, block * cells_y : (block + 1) * cells_y], blocks[block])
            for block in range(half)
        )
        extra_made[:, lanes] = extra
        extra_copy(part).start()
        value = sum(
            dot_rows(table[:, :, block * cells_y : (block + 1) * cells_y], blocks[block])
            for block in range(half)
        )
        made[:, :, :, lanes] = value.reshape(strike_count, 2, band, chunk)

        @pl.loop(0, steps // CHUNKS)
        def _(step):
            memory_step(part * (steps // CHUNKS) + step)

        extra_copy(part).wait()
        keep = jnp.where(place == 0, 1.0, 0.0)
        for source in range(strike_count):
            for side_part in range(2):
                at = 2 * source + side_part
                made[source, side_part, 0:1, lanes] = (
                    made[source, side_part, 0:1, lanes] + keep * extra_held[at : at + 1, lanes]
                )
        own_copy(part).start()

        @pl.loop(1, strike_count)
        def _(offset):
            band_copy(offset, part).start()

    @pl.loop(0, CHUNKS)
    def _(part):
        own_copy(part).wait()

        @pl.loop(1, strike_count)
        def _(offset):
            band_copy(offset, part).wait()

    def back_copy(offset, block):
        lines = pl.ds(pl.multiple_of(block * SUB, SUB), SUB)
        target = (me + offset) % group
        return pltpu.make_async_remote_copy(
            src_ref=sent.at[target, :, lines],
            dst_ref=back_out.at[me, :, lines],
            send_sem=back_sem.at[0, offset - 1, block],
            recv_sem=back_sem.at[1, offset - 1, block],
            device_id=in_half(target),
            device_id_type=MESH,
        )

    def back_own_copy(block):
        lines = pl.ds(pl.multiple_of(block * SUB, SUB), SUB)
        return pltpu.make_async_copy(
            sent.at[me, :, lines], back_out.at[me, :, lines], back_own_sem.at[block]
        )

    @pl.loop(0, band // SUB)
    def _(block):
        lines = pl.ds(pl.multiple_of(block * SUB, SUB), SUB)

        def load(source, part):
            return jnp.stack(
                [
                    held[source, part, lines, tile * INNER : (tile + 1) * INNER]
                    for tile in range(tiles)
                ]
            )

        forward(load, turns_in, twists_in, spectrum, grid, strike_count)
        for part in range(2):
            for at in range(outer):
                natural[part, at * SUB : (at + 1) * SUB, :] = memory[
                    part, lines, at * INNER : (at + 1) * INNER
                ]
            reorder(natural.at[part], mixed.at[part], outer)
        shape = (outer * SUB, INNER)
        line = lax.broadcasted_iota(jnp.int32, shape, 0)
        lane = lax.broadcasted_iota(jnp.int32, shape, 1)
        mode_x = line // SUB + lane // outer * outer + lane % outer * INNER
        row = line % SUB + block * SUB
        wave_x = wavenumber(mode_x, total_x)
        wave_y = wavenumber((strike * dip_count + dip) * band + row, total_y)
        times = jnp.where((row == 0) & (place == 0), 1.0, 2.0)
        static = (-0.5 * shear_modulus) * times * jnp.sqrt(wave_y * wave_y + wave_x * wave_x)
        spectrum[:, :INNER] = static * spectrum[:, :INNER] + mixed[0]
        spectrum[:, INNER:] = static * spectrum[:, INNER:] + mixed[1]
        share = tiles // half

        def store(source, part, value):
            for tile in range(tiles):
                lanes = slice(tile % share * INNER, (tile % share + 1) * INNER)
                sent[source * half + tile // share, part, lines, lanes] = value[tile]

        backward(store, turns_in, twists_in, spectrum, grid, strike_count)
        back_own_copy(block).start()

        @pl.loop(1, group)
        def _(offset):
            back_copy(offset, block).start()

    taken = table_held.shape[2] // (2 * band)
    shares = strike_count // taken
    rate_steps = half * shares

    def table_copy(step, slot):
        lines = pl.ds(pl.multiple_of(step % shares * taken * 2 * band, 2 * SUB), taken * 2 * band)
        return pltpu.make_async_copy(
            table_all.at[side, :, step // shares, lines], table_held.at[slot], table_sem.at[slot]
        )

    def rate_out_copy(step, slot):
        lines = pl.ds(step % shares * taken, taken)
        return pltpu.make_async_copy(
            rate_made.at[slot], rate_out.at[lines, step // shares], rate_out_sem.at[slot]
        )

    table_copy(0, 0).start()
    for turn in range(1, dip_count):
        rate_copy(turn).wait()
    for turn in range(dip_count):
        block = (dip + dip_count - turn) % dip_count
        lines = pl.ds(pl.multiple_of(block * cells_y, INNER), cells_y)
        value = rate_held[turn].T
        high = value.astype(jnp.bfloat16)
        joined[0, lines] = high
        joined[1, lines] = (value - high.astype(jnp.float32)).astype(jnp.bfloat16)

    @pl.loop(0, rate_steps)
    def _(step):
        slot = step % 2

        @pl.when(step + 1 < rate_steps)
        def _():
            table_copy(step + 1, 1 - slot).start()

        table_copy(step, slot).wait()

        @pl.when(step >= 2)
        def _():
            rate_out_copy(step - 2, slot).wait()

        dot = functools.partial(jnp.dot, preferred_element_type=jnp.float32)
        first, second = table_held[slot, 0], table_held[slot, 1]
        value = dot(first, joined[0]) + (dot(first, joined[1]) + dot(second, joined[0]))
        rate_made[slot] = value.reshape(taken, 2, band, rows)
        rate_out_copy(step, slot).start()

    for step in range(rate_steps - 2, rate_steps):
        rate_out_copy(step, step % 2).wait()

    @pl.loop(0, band // SUB)
    def _(block):
        back_own_copy(block).wait()

        @pl.loop(1, group)
        def _(offset):
            back_copy(offset, block).wait()


def stress_back(strike_count, dip_count, slip, rate, kernel, history, tables, turns, twists):
    half = dip_count // 2
    cells_x, cells_y = slip.shape
    lags, band, total_x = kernel.shape
    total_y = cells_y * dip_count
    rows = cells_x // half
    group = strike_count * half
    outer = total_x // INNER
    chunk = cells_x // CHUNKS
    depth = 2 * SUB
    parts = max(4, CHUNKS * depth // band)
    taken = 2
    lines = strike_count * 2 * band
    assert INNER == 2 * outer and band % depth == 0 and chunk % INNER == 0
    f32, b16, dma = jnp.float32, jnp.bfloat16, pltpu.SemaphoreType.DMA
    whole = pl.BlockSpec(memory_space=pl.ANY)
    size = band * total_x
    return pl.pallas_call(
        functools.partial(stress_kernel, strike_count, dip_count),
        out_shape=[
            jax.ShapeDtypeStruct((group, 2, band, rows), f32),
            jax.ShapeDtypeStruct((strike_count, half, 2, band, rows), f32),
        ],
        in_specs=[whole] * 6 + [pl.BlockSpec(memory_space=pltpu.VMEM)] * 2,
        out_specs=[whole] * 2,
        scratch_shapes=[
            pltpu.VMEM((half, cells_x, cells_y), f32),
            pltpu.VMEM((strike_count, 2, band, cells_x), f32),
            pltpu.VMEM((strike_count, 2, band, cells_x), f32),
            pltpu.VMEM((group, 2, band, rows), f32),
            pltpu.VMEM((2, lines, half * cells_y), b16),
            pltpu.VMEM((2, strike_count * 2, half * cells_y), b16),
            pltpu.VMEM((strike_count * 2, cells_x), f32),
            pltpu.VMEM((strike_count * 2, cells_x), f32),
            pltpu.VMEM((2, lags, depth, total_x // parts), b16),
            pltpu.VMEM((2, lags, 2, depth, total_x // parts), b16),
            pltpu.VMEM((2, band, total_x), f32),
            pltpu.VMEM((outer * SUB, 2 * INNER), f32),
            pltpu.VMEM((2, strike_count, outer // strike_count, SUB, INNER), f32),
            pltpu.VMEM((2, outer * SUB, INNER), f32),
            pltpu.VMEM((2, outer * SUB, INNER), f32),
            pltpu.VMEM((dip_count, rows, cells_y), f32),
            pltpu.VMEM((2, total_y, rows), b16),
            pltpu.VMEM((2, 2, taken * 2 * band, total_y), b16),
            pltpu.VMEM((2, taken, 2, band, rows), f32),
            dma((4,)),
            dma((2,)),
            dma((2,)),
            dma((2, 2)),
            dma((2, max(1, half - 1), CHUNKS)),
            dma((2, CHUNKS)),
            dma((2, strike_count - 1, CHUNKS)),
            dma((CHUNKS,)),
            dma((2, dip_count - 1)),
            dma((2, group - 1, band // SUB)),
            dma((band // SUB,)),
        ],
        compiler_params=pltpu.CompilerParams(
            vmem_limit_bytes=56 * 1024 * 1024, collective_id=0, has_side_effects=True
        ),
        cost_estimate=pl.CostEstimate(
            flops=size * 8000, bytes_accessed=size * 120, transcendentals=size
        ),
    )(slip, rate, kernel, history, *tables, turns, twists)


def line_kernel(where_in, back, table, out):
    half = back.shape[1]
    total = None
    for place in range(half):
        value = back[:, place].reshape(-1, back.shape[3])
        high = value.astype(jnp.bfloat16)
        low = (value - high.astype(jnp.float32)).astype(jnp.bfloat16)

        def dot(left, right):
            return lax.dot_general(
                left, right, (((0,), (0,)), ((), ())), preferred_element_type=jnp.float32
            )

        first, second = table[0, 0, place], table[0, 1, place]
        value = dot(high, first) + (dot(low, first) + dot(high, second))
        total = value if total is None else total + value
    out[...] = total


def line_piece(where, back, table, cells_y):
    _, _, half, lines, total_y = table.shape
    strike_count, _, both, rows = back.shape
    return pl.pallas_call(
        line_kernel,
        out_shape=jax.ShapeDtypeStruct((rows, cells_y), jnp.float32),
        grid_spec=pltpu.PrefetchScalarGridSpec(
            num_scalar_prefetch=1,
            grid=(1,),
            in_specs=[
                pl.BlockSpec(back.shape, lambda step, where: (0, 0, 0, 0)),
                pl.BlockSpec(
                    (1, 2, half, lines, cells_y),
                    lambda step, where: (where[0], 0, 0, 0, where[3]),
                ),
            ],
            out_specs=pl.BlockSpec((rows, cells_y), lambda step, where: (0, 0)),
        ),
        compiler_params=pltpu.CompilerParams(vmem_limit_bytes=48 * 1024 * 1024),
        cost_estimate=pl.CostEstimate(
            flops=6 * half * lines * rows * cells_y,
            bytes_accessed=8 * half * lines * rows,
            transcendentals=0,
        ),
    )(where, back, table)


def modes_kernel(strike_count, piece_in, turns_in, twists_in, out, spectrum, grid, natural, mixed):
    outer = twists_in.shape[2]
    tiles = outer // strike_count
    share = piece_in.shape[3] // INNER
    groups = piece_in.shape[2] // SUB
    for group in range(groups):
        lines = slice(group * SUB, (group + 1) * SUB)

        def load(source, part):
            places = [(source * tiles + tile) // share for tile in range(tiles)]
            offsets = [(source * tiles + tile) % share * INNER for tile in range(tiles)]
            return jnp.stack(
                [
                    piece_in[place, part, lines, offset : offset + INNER]
                    for place, offset in zip(places, offsets)
                ]
            )

        forward(load, turns_in, twists_in, spectrum, grid, strike_count)
        for part in range(2):
            natural[part] = spectrum[:, part * INNER : (part + 1) * INNER]
            reorder(natural.at[part], mixed.at[group, part], outer)
    for part in range(2):
        for at in range(outer):
            lines = slice(at * SUB, (at + 1) * SUB)
            tile = jnp.concatenate([mixed[group, part, lines, :] for group in range(groups)], 0)
            out[part, :, at * INNER : (at + 1) * INNER] = tile.astype(jnp.bfloat16)


def modes(strike_count, piece, turns, twists):
    sources, _, band, chunk = piece.shape
    total = sources * chunk
    outer = total // INNER
    lines = 2 * SUB
    assert INNER == 2 * outer and band % lines == 0
    size = band * total
    return pl.pallas_call(
        functools.partial(modes_kernel, strike_count),
        grid=(band // lines,),
        out_shape=jax.ShapeDtypeStruct((2, band, total), jnp.bfloat16),
        in_specs=[
            pl.BlockSpec((sources, 2, lines, chunk), lambda step: (0, 0, step, 0)),
            pl.BlockSpec(turns.shape, lambda step: (0,) * 4),
            pl.BlockSpec(twists.shape, lambda step: (0,) * 5),
        ],
        out_specs=pl.BlockSpec((2, lines, total), lambda step: (0, step, 0)),
        scratch_shapes=[
            pltpu.VMEM((outer * SUB, 2 * INNER), jnp.float32),
            pltpu.VMEM((2, strike_count, outer // strike_count, SUB, INNER), jnp.float32),
            pltpu.VMEM((2, outer * SUB, INNER), jnp.float32),
            pltpu.VMEM((2, 2, outer * SUB, INNER), jnp.float32),
        ],
        compiler_params=pltpu.CompilerParams(vmem_limit_bytes=32 * 1024 * 1024),
        cost_estimate=pl.CostEstimate(
            flops=size * 2000, bytes_accessed=size * 12, transcendentals=0
        ),
    )(piece, turns, twists)


def per_device(
    slip,
    slip_rate,
    state,
    loading,
    normal_stress,
    patch,
    rate_coef,
    state_coef,
    slip_scale,
    kernel,
    history,
):
    strike_count = lax.axis_size("strike")
    dip_count = lax.axis_size("dip")
    half = dip_count // 2
    both_axes = ("strike", "dip")
    cells_x, cells_y = slip.shape
    band, total_x = kernel.shape[1:]
    total_y = cells_y * dip_count
    rows = cells_x // half
    strike, dip = lax.axis_index("strike"), lax.axis_index("dip")
    side, place = dip // half, dip % half
    sides = [
        [s * dip_count + t * half + k for s in range(strike_count) for k in range(half)]
        for t in range(2)
    ]

    def across_half(array):
        return lax.all_to_all(
            array, both_axes, split_axis=0, concat_axis=0, tiled=True, axis_index_groups=sides
        )

    def turn_dip(array, turn):
        return lax.ppermute(array, "dip", [(d, (d + turn) % dip_count) for d in range(dip_count)])

    turns, twists = (jnp.asarray(value) for value in strike_tables(total_x, strike_count))
    tables = [jnp.asarray(value) for value in dip_tables(strike_count, dip_count, band, total_y)]
    back, rate_parts = stress_back(
        strike_count, dip_count, slip, slip_rate, kernel, history, tables, turns, twists
    )
    back = back.reshape(strike_count, half, 2 * band, rows)
    cells = (slip_rate, state, loading, normal_stress, patch)

    def where(turn):
        return jnp.stack([side, dip, place, (dip + turn) % dip_count])

    pieces = {}
    for turn in sorted(range(dip_count), key=lambda turn: (turn == 0, turn % half, turn < half)):
        piece = line_piece(where(turn), back, tables[0], cells_y)
        pieces[turn] = turn_dip(piece, turn) if turn else piece
    rate_both = across_half(rate_parts.reshape(-1, 2, band, rows))
    rate_modes = modes(strike_count, rate_both, turns, twists)
    outs = []
    for turn in range(half):
        outs = friction(
            ((dip + dip_count - turn) % half).reshape(1),
            (rate_coef, state_coef, slip_scale),
            (pieces[turn], pieces[turn + half]),
            cells,
            [rate_modes] if turn else [],
            outs,
        )
    return (*outs, rate_modes)


def solution(mesh):
    return jax.shard_map(
        per_device,
        mesh=mesh,
        in_specs=(
            P("strike", "dip"),
            P("strike", "dip"),
            P("strike", "dip"),
            P("strike", "dip"),
            P("strike", "dip"),
            P("strike", "dip"),
            P(),
            P(),
            P(),
            P(None, ("strike", "dip"), None),
            P(None, None, ("strike", "dip"), None),
        ),
        out_specs=(
            P("strike", "dip"),
            P("strike", "dip"),
            P("strike", "dip"),
            P(None, ("strike", "dip"), None),
        ),
        check_vma=False,
    )
```

```python
import functools
import math

import jax
import jax.numpy as jnp
import numpy as np
from jax import lax
from jax.experimental import pallas as pl
from jax.experimental.pallas import tpu as pltpu
from jax.sharding import PartitionSpec as P

NEWTON = 8


shear_modulus = 1.0
damping = 0.5
relaxation = 0.35
time_step = 0.1


def inverse_sinh(value):
    size_v = jnp.abs(value)
    square = size_v * size_v
    result = jnp.log1p(size_v + square / (1.0 + jnp.sqrt(square + 1.0)))
    return jnp.where(value < 0.0, -result, result)


INNER = 128
SUB = 8
CHUNKS = 4
EARLY_PART = 2
MESH = pl.DeviceIdType.MESH


def wavenumber(index, count):
    return 2.0 * math.pi / count * ((index + count // 2) % count - count // 2).astype(jnp.float32)


def friction_kernel(
    labels,
    filled,
    where_in,
    rate_coef,
    state_coef,
    slip_scale,
    transfer_in,
    transfer_add,
    slip_rate_in,
    state_in,
    loading_in,
    normal_in,
    patch_in,
    *refs,
):
    new_rate_out, new_state_out, transfer_out = refs[filled:]
    patch = patch_in[...]

    def choose(table):
        result = jnp.zeros(patch.shape, jnp.float32)
        for label in range(labels):
            result = jnp.where(patch == label, table[label], result)
        return result

    coef_a = choose(rate_coef)
    coef_b = choose(state_coef)
    length_l = choose(slip_scale)
    transfer = transfer_in[...] + transfer_add[...]
    state = state_in[...]
    stress = loading_in[...] + transfer
    prefix = 2.0 * jnp.exp(-state / coef_a)
    angle_w = inverse_sinh(slip_rate_in[...] / prefix)
    weight = normal_in[...] * coef_a
    half = 0.5 * damping * prefix
    for iteration in range(NEWTON):
        raised = jnp.exp(angle_w)
        square = raised * raised
        residue = half * (square - 1.0) + (weight * angle_w - stress) * raised
        slope = half * (square + 1.0) + weight * raised
        angle_w = angle_w - relaxation * residue / (slope + jnp.abs(residue))
    new_rate = (0.5 * prefix) * (jnp.exp(angle_w) - jnp.exp(-angle_w))
    new_rate_out[...] = new_rate
    new_state_out[...] = state + time_step * (coef_b / length_l) * (
        jnp.exp(-state / coef_b) - jnp.abs(new_rate)
    )
    transfer_out[...] = transfer


def friction(where, tables, transfers, cells, earlier, before):
    rows, columns = transfers[0].shape
    blocks = 2
    step_rows = rows // blocks
    block = pl.BlockSpec((step_rows, columns), lambda step, where: (where[0] * blocks + step, 0))
    local = pl.BlockSpec((step_rows, columns), lambda step, where: (step, 0))
    scalar = pl.BlockSpec(memory_space=pltpu.SMEM)
    size = rows * columns
    first = 1 + len(tables) + 2 + len(cells) + len(earlier)
    kept = len(earlier) + len(before)
    return pl.pallas_call(
        functools.partial(friction_kernel, tables[0].shape[0], kept),
        out_shape=[jax.ShapeDtypeStruct(cells[0].shape, jnp.float32)] * 3,
        grid_spec=pltpu.PrefetchScalarGridSpec(
            num_scalar_prefetch=1,
            grid=(blocks,),
            in_specs=[scalar] * len(tables)
            + [local] * 2
            + [block] * len(cells)
            + [pl.BlockSpec(memory_space=pl.ANY)] * kept,
            out_specs=[block] * 3,
        ),
        input_output_aliases={first + index: index for index in range(len(before))},
        compiler_params=pltpu.CompilerParams(vmem_limit_bytes=32 * 1024 * 1024),
        cost_estimate=pl.CostEstimate(
            flops=size * 200, bytes_accessed=size * 40, transcendentals=size * 30
        ),
    )(where, *tables, *transfers, *cells, *earlier, *before)


def split_parts(value):
    high = value.astype(jnp.bfloat16)
    return np.stack([high, (value - high.astype(np.float32)).astype(jnp.bfloat16)])


def dip_tables(strike_count, dip_count, band, total):
    half = dip_count // 2
    index = np.arange(total).reshape(strike_count, 2, half, band).transpose(1, 2, 0, 3)
    turn = index[..., None] * np.arange(total) % total * (2.0 * np.pi / total)
    table = np.stack([np.cos(turn), -np.sin(turn)], 3) / math.sqrt(total)
    mirrored = table[:, 0, :, :, 0].reshape(2, strike_count * 2, total)
    table = table.reshape(2, half, strike_count * 2 * band, total)
    return [
        np.ascontiguousarray(np.moveaxis(split_parts(part.astype(np.float32)), 0, 1))
        for part in (table, mirrored)
    ]


def lane_order(outer):
    fold = INNER // outer
    return (np.arange(outer)[None, :] * fold + np.arange(fold)[:, None]).reshape(-1)


def strike_tables(total, sources):
    outer = total // INNER
    order = lane_order(outer)
    turn = np.arange(INNER)[:, None] * order[None, :] % INNER * (2.0 * np.pi / INNER)
    cos, sin = np.cos(turn) / math.sqrt(total), np.sin(turn) / math.sqrt(total)
    there = np.block([[cos, -sin], [sin, cos]])
    back = np.block([[cos.T, sin.T], [-sin.T, cos.T]])
    both = np.stack([there, back]).astype(np.float32)
    high = both.astype(jnp.bfloat16)
    low = (both - high.astype(np.float32)).astype(jnp.bfloat16)
    twist = np.arange(outer)[:, None] * np.arange(INNER)[None, :] * (2.0 * np.pi / total)
    twist = np.stack([np.cos(twist), np.sin(twist)])
    tiles = outer // sources
    small = np.arange(sources)[:, None] * np.arange(tiles)[None, :] * (2.0 * np.pi / outer)
    small = np.stack([np.cos(small), np.sin(small)]).reshape(2, outer)
    twists = np.stack([twist, np.broadcast_to(small[:, :, None], twist.shape)])
    twists = np.broadcast_to(twists[:, :, :, None, :], (2, 2, outer, SUB, INNER))
    return np.stack([high, low], 1), np.ascontiguousarray(twists.astype(np.float32))


def times_root(value, step, count, sign):
    re, im = value
    if step == 0:
        return re, im
    if 4 * step == count:
        return (-im, re) if sign > 0 else (im, -re)
    if 8 * step == count or 8 * step == 3 * count:
        root = math.sqrt(0.5)
        if sign > 0:
            turned = (re - im, re + im) if 8 * step == count else (-re - im, re - im)
        else:
            turned = (re + im, im - re) if 8 * step == count else (im - re, -re - im)
        return turned[0] * root, turned[1] * root
    cos = math.cos(2.0 * math.pi * step / count)
    sin = sign * math.sin(2.0 * math.pi * step / count)
    return re * cos - im * sin, re * sin + im * cos


def short_transform(values, sign):
    count = len(values)
    if count == 1:
        return values
    even = short_transform(values[0::2], sign)
    odd = short_transform(values[1::2], sign)
    low, high = [], []
    for step in range(count // 2):
        turned = times_root(odd[step], step, count, sign)
        low.append((even[step][0] + turned[0], even[step][1] + turned[1]))
        high.append((even[step][0] - turned[0], even[step][1] - turned[1]))
    return low + high


def exact_dot(left, table):
    high = left.astype(jnp.bfloat16)
    low = (left - high.astype(jnp.float32)).astype(jnp.bfloat16)
    dot = functools.partial(jnp.dot, preferred_element_type=jnp.float32)
    return dot(high, table[0]) + (dot(low, table[0]) + dot(high, table[1]))


def forward(load, turns_in, twists_in, spectrum, grid, sources):
    outer = twists_in.shape[2]
    tiles = outer // sources
    values = [(load(source, 0), load(source, 1)) for source in range(sources)]
    for at, (re, im) in enumerate(short_transform(values, -1.0)):
        lines = slice(at * tiles, (at + 1) * tiles)
        cos, sin = twists_in[1, 0, lines], twists_in[1, 1, lines]
        grid[0, at] = re * cos + im * sin
        grid[1, at] = im * cos - re * sin
    values = [(grid[0, :, tile], grid[1, :, tile]) for tile in range(tiles)]
    for at, (re, im) in enumerate(short_transform(values, -1.0)):
        lines = slice(at * sources, (at + 1) * sources)
        cos, sin = twists_in[0, 0, lines], twists_in[0, 1, lines]
        lines = slice(at * sources * SUB, (at + 1) * sources * SUB)
        spectrum[lines, :INNER] = (re * cos + im * sin).reshape(-1, INNER)
        spectrum[lines, INNER:] = (im * cos - re * sin).reshape(-1, INNER)
    spectrum[...] = exact_dot(spectrum[...], turns_in[0])


def backward(store, turns_in, twists_in, spectrum, grid, sources):
    outer = twists_in.shape[2]
    tiles = outer // sources
    spectrum[...] = exact_dot(spectrum[...], turns_in[1])
    values = []
    for at in range(tiles):
        lines = slice(at * sources * SUB, (at + 1) * sources * SUB)
        re = spectrum[lines, :INNER].reshape(sources, SUB, INNER)
        im = spectrum[lines, INNER:].reshape(sources, SUB, INNER)
        lines = slice(at * sources, (at + 1) * sources)
        cos, sin = twists_in[0, 0, lines], twists_in[0, 1, lines]
        values.append((re * cos - im * sin, re * sin + im * cos))
    for tile, (re, im) in enumerate(short_transform(values, 1.0)):
        grid[0, :, tile] = re
        grid[1, :, tile] = im
    values = []
    for at in range(sources):
        lines = slice(at * tiles, (at + 1) * tiles)
        cos, sin = twists_in[1, 0, lines], twists_in[1, 1, lines]
        re, im = grid[0, at], grid[1, at]
        values.append((re * cos - im * sin, re * sin + im * cos))
    for source, pair in enumerate(short_transform(values, 1.0)):
        for part in range(2):
            store(source, part, pair[part])


def reorder(source, target, outer):
    lane = lax.broadcasted_iota(jnp.int32, (outer, INNER), 1)
    for row in range(0, SUB, 2):
        pair = [source[pl.ds(row + at, outer, stride=SUB), :] for at in range(2)]
        turned = jnp.concatenate(pair, 0).T
        upper, lower = turned[:outer], turned[outer:]
        first = jnp.where(lane < outer, upper, pltpu.roll(lower, outer, 1))
        second = jnp.where(lane < outer, pltpu.roll(upper, outer, 1), lower)
        target[pl.ds(row, outer, stride=SUB), :] = first
        target[pl.ds(row + 1, outer, stride=SUB), :] = second


def dot_rows(table, value):
    high = value.astype(jnp.bfloat16)
    low = (value - high.astype(jnp.float32)).astype(jnp.bfloat16)

    def dot(left, right):
        return lax.dot_general(
            left, right, (((1,), (1,)), ((), ())), preferred_element_type=jnp.float32
        )

    return dot(table[0], high) + (dot(table[0], low) + dot(table[1], high))


def stress_kernel(
    strike_count,
    dip_count,
    slip,
    rate,
    kernel,
    history,
    table_all,
    mirror_all,
    turns_in,
    twists_in,
    back_out,
    rate_out,
    slip_held,
    made,
    held,
    sent,
    table,
    mirror,
    extra_made,
    extra_held,
    extra_parts,
    kernel_held,
    history_held,
    memory,
    spectrum,
    grid,
    natural,
    mixed,
    rate_held,
    joined,
    table_held,
    rate_made,
    local_sem,
    table_sem,
    rate_out_sem,
    memory_sem,
    slip_sem,
    extra_sem,
    extra_part_sem,
    band_sem,
    own_sem,
    rate_sem,
    back_sem,
    back_own_sem,
):
    half = dip_count // 2
    strike, dip = lax.axis_index("strike"), lax.axis_index("dip")
    side, place = dip // half, dip % half
    cells_x, cells_y = slip.shape
    lags, _, band, total_x = history.shape
    total_y = cells_y * dip_count
    rows = cells_x // half
    group = strike_count * half
    me = strike * half + place
    chunk = cells_x // CHUNKS
    outer = total_x // INNER
    tiles = outer // strike_count

    def in_half(index):
        return (index // half, side * half + index % half)

    barrier = pltpu.get_barrier_semaphore()

    @pl.loop(1, group)
    def _(offset):
        pl.semaphore_signal(
            barrier, inc=1, device_id=in_half((me + offset) % group), device_id_type=MESH
        )

    for other in range(half):
        pl.semaphore_signal(
            barrier,
            inc=1,
            device_id=(strike, (1 - side) * half + other),
            device_id_type=MESH,
        )
    pl.semaphore_wait(barrier, group - 1 + half)

    def slip_copy(offset, part):
        lines = pl.ds(part * chunk, chunk)
        return pltpu.make_async_remote_copy(
            src_ref=slip.at[lines],
            dst_ref=slip_held.at[place, lines],
            send_sem=slip_sem.at[0, offset - 1, part],
            recv_sem=slip_sem.at[1, offset - 1, part],
            device_id=(strike, side * half + (place + offset) % half),
            device_id_type=MESH,
        )

    for part in range(CHUNKS):
        for offset in range(1, half):
            slip_copy(offset, part).start()
    columns = pl.ds(pl.multiple_of(side * half * cells_y, INNER), half * cells_y)
    firsts = [
        pltpu.make_async_copy(slip, slip_held.at[place], local_sem.at[0]),
        pltpu.make_async_copy(table_all.at[side, :, place, :, columns], table, local_sem.at[1]),
        pltpu.make_async_copy(mirror_all.at[1 - side, :, :, columns], mirror, local_sem.at[2]),
        pltpu.make_async_copy(
            rate.at[pl.ds(pl.multiple_of(place * rows, SUB), rows)], rate_held.at[0], local_sem.at[3]
        ),
    ]
    for copy in firsts:
        copy.start()

    depth, width = kernel_held.shape[2:]
    across = total_x // width
    steps = band // depth * across

    def memory_copies(step, slot):
        lines = pl.ds(pl.multiple_of(step // across * depth, depth), depth)
        lanes = pl.ds(pl.multiple_of(step % across * width, width), width)
        return (
            pltpu.make_async_copy(
                kernel.at[:, lines, lanes], kernel_held.at[slot], memory_sem.at[0, slot]
            ),
            pltpu.make_async_copy(
                history.at[:, :, lines, lanes], history_held.at[slot], memory_sem.at[1, slot]
            ),
        )

    for copy in memory_copies(0, 0):
        copy.start()

    def memory_step(step):
        slot = step % 2

        @pl.when(step + 1 < steps)
        def _():
            for copy in memory_copies(step + 1, 1 - slot):
                copy.start()

        for copy in memory_copies(step, slot):
            copy.wait()
        piece = 2 * INNER

        @pl.loop(0, width // piece)
        def _(at):
            lanes = pl.ds(pl.multiple_of(at * piece, piece), piece)
            sums = [jnp.zeros((depth, piece), jnp.float32) for _ in range(2)]
            for lag in range(lags):
                factor = kernel_held[slot, lag, :, lanes].astype(jnp.float32)
                for part in range(2):
                    past = history_held[slot, lag, part, :, lanes].astype(jnp.float32)
                    sums[part] = sums[part] + factor * past
            lines = pl.ds(pl.multiple_of(step // across * depth, depth), depth)
            lanes = pl.ds(pl.multiple_of(step % across * width + at * piece, piece), piece)
            for part in range(2):
                memory[part, lines, lanes] = sums[part]

    def rate_copy(turn):
        target = (dip + turn) % dip_count
        lines = pl.ds(pl.multiple_of(target % half * rows, SUB), rows)
        return pltpu.make_async_remote_copy(
            src_ref=rate.at[lines],
            dst_ref=rate_held.at[turn],
            send_sem=rate_sem.at[0, turn - 1],
            recv_sem=rate_sem.at[1, turn - 1],
            device_id=(strike, target),
            device_id_type=MESH,
        )

    def extra_copy():
        return pltpu.make_async_remote_copy(
            src_ref=extra_made,
            dst_ref=extra_held,
            send_sem=extra_sem.at[0],
            recv_sem=extra_sem.at[1],
            device_id=(strike, (dip + half) % dip_count),
            device_id_type=MESH,
        )

    def extra_part_copy(offset):
        target = (strike + offset) % strike_count
        return pltpu.make_async_remote_copy(
            src_ref=extra_held.at[pl.ds(2 * target, 2)],
            dst_ref=extra_parts.at[strike],
            send_sem=extra_part_sem.at[0, offset - 1],
            recv_sem=extra_part_sem.at[1, offset - 1],
            device_id=(target, dip),
            device_id_type=MESH,
        )

    def band_copy(offset, part):
        lanes = pl.ds(pl.multiple_of(part * chunk, INNER), chunk)
        target = (strike + offset) % strike_count
        return pltpu.make_async_remote_copy(
            src_ref=made.at[target, :, :, lanes],
            dst_ref=held.at[strike, :, :, lanes],
            send_sem=band_sem.at[0, offset - 1, part],
            recv_sem=band_sem.at[1, offset - 1, part],
            device_id=(target, dip),
            device_id_type=MESH,
        )

    def own_copy(part):
        lanes = pl.ds(pl.multiple_of(part * chunk, INNER), chunk)
        return pltpu.make_async_copy(
            made.at[strike, :, :, lanes], held.at[strike, :, :, lanes], own_sem.at[part]
        )

    def start_rate(turn, early):
        middle = ((dip == half - 1) & (turn == 1)) | ((dip == half) & (turn == dip_count - 1))

        @pl.when(middle == early)
        def _():
            rate_copy(turn).start()

    for turn in range(1, dip_count):
        start_rate(turn, True)
    for copy in firsts:
        copy.wait()

    @pl.loop(0, CHUNKS)
    def _(part):
        @pl.loop(0, steps // CHUNKS)
        def _(step):
            memory_step(part * (steps // CHUNKS) + step)

        for offset in range(1, half):
            slip_copy(offset, part).wait()

        @pl.when(part == CHUNKS - 1)
        def _():
            for turn in range(1, dip_count):
                start_rate(turn, False)

        lines = pl.ds(pl.multiple_of(part * chunk, SUB), chunk)
        lanes = pl.ds(pl.multiple_of(part * chunk, INNER), chunk)
        blocks = [slip_held[block, lines] for block in range(half)]
        extra = sum(
            dot_rows(mirror[:, :, block * cells_y : (block + 1) * cells_y], blocks[block])
            for block in range(half)
        )
        for tile in range(chunk // INNER):
            for at in range(2 * strike_count):
                extra_made[at, pl.ds(part * (chunk // INNER) + tile, 1), :] = extra[
                    at : at + 1, tile * INNER : (tile + 1) * INNER
                ]
        value = sum(
            dot_rows(table[:, :, block * cells_y : (block + 1) * cells_y], blocks[block])
            for block in range(half)
        )
        made[:, :, :, lanes] = value.reshape(strike_count, 2, band, chunk)

        own_copy(part).start()

        @pl.loop(1, strike_count)
        def _(offset):
            band_copy(offset, part).start()

    extra_copy().start()
    extra_copy().wait()

    @pl.loop(1, strike_count)
    def _(offset):
        extra_part_copy(offset).start()

    own_extra = pltpu.make_async_copy(
        extra_held.at[pl.ds(2 * strike, 2)], extra_parts.at[strike], local_sem.at[0]
    )
    own_extra.start()

    @pl.loop(0, CHUNKS)
    def _(part):
        own_copy(part).wait()

        @pl.loop(1, strike_count)
        def _(offset):
            band_copy(offset, part).wait()

    own_extra.wait()

    @pl.loop(1, strike_count)
    def _(offset):
        extra_part_copy(offset).wait()

    keep = jnp.where(place == 0, 1.0, 0.0)

    @pl.loop(0, strike_count)
    def _(source):
        for side_part in range(2):
            for tile in range(tiles):
                lanes = slice(tile * INNER, (tile + 1) * INNER)
                held[source, side_part, 0:1, lanes] = (
                    held[source, side_part, 0:1, lanes]
                    + keep * extra_parts[source, side_part, tile : tile + 1, :]
                )

    def back_copy(offset, block):
        lines = pl.ds(pl.multiple_of(block * SUB, SUB), SUB)
        target = (me + offset) % group
        return pltpu.make_async_remote_copy(
            src_ref=sent.at[target, :, lines],
            dst_ref=back_out.at[me, :, lines],
            send_sem=back_sem.at[0, offset - 1, block],
            recv_sem=back_sem.at[1, offset - 1, block],
            device_id=in_half(target),
            device_id_type=MESH,
        )

    def back_own_copy(block):
        lines = pl.ds(pl.multiple_of(block * SUB, SUB), SUB)
        return pltpu.make_async_copy(
            sent.at[me, :, lines], back_out.at[me, :, lines], back_own_sem.at[block]
        )

    def send_back(block):
        back_own_copy(block).start()

        @pl.loop(1, group)
        def _(offset):
            back_copy(offset, block).start()

    early = band // SUB // EARLY_PART

    @pl.loop(0, band // SUB)
    def _(block):
        lines = pl.ds(pl.multiple_of(block * SUB, SUB), SUB)

        def load(source, part):
            return jnp.stack(
                [
                    held[source, part, lines, tile * INNER : (tile + 1) * INNER]
                    for tile in range(tiles)
                ]
            )

        forward(load, turns_in, twists_in, spectrum, grid, strike_count)
        for part in range(2):
            for at in range(outer):
                natural[part, at * SUB : (at + 1) * SUB, :] = memory[
                    part, lines, at * INNER : (at + 1) * INNER
                ]
            reorder(natural.at[part], mixed.at[part], outer)
        shape = (outer * SUB, INNER)
        line = lax.broadcasted_iota(jnp.int32, shape, 0)
        lane = lax.broadcasted_iota(jnp.int32, shape, 1)
        mode_x = line // SUB + lane // outer * outer + lane % outer * INNER
        row = line % SUB + block * SUB
        wave_x = wavenumber(mode_x, total_x)
        wave_y = wavenumber((strike * dip_count + dip) * band + row, total_y)
        times = jnp.where((row == 0) & (place == 0), 1.0, 2.0)
        static = (-0.5 * shear_modulus) * times * jnp.sqrt(wave_y * wave_y + wave_x * wave_x)
        spectrum[:, :INNER] = static * spectrum[:, :INNER] + mixed[0]
        spectrum[:, INNER:] = static * spectrum[:, INNER:] + mixed[1]
        share = tiles // half

        def store(source, part, value):
            for tile in range(tiles):
                lanes = slice(tile % share * INNER, (tile % share + 1) * INNER)
                sent[source * half + tile // share, part, lines, lanes] = value[tile]

        backward(store, turns_in, twists_in, spectrum, grid, strike_count)
        @pl.when(block < early)
        def _():
            send_back(block)

    taken = table_held.shape[2] // (2 * band)
    shares = strike_count // taken
    rate_steps = half * shares

    def table_copy(step, slot):
        lines = pl.ds(pl.multiple_of(step % shares * taken * 2 * band, 2 * SUB), taken * 2 * band)
        return pltpu.make_async_copy(
            table_all.at[side, :, step // shares, lines], table_held.at[slot], table_sem.at[slot]
        )

    def rate_out_copy(step, slot):
        lines = pl.ds(step % shares * taken, taken)
        return pltpu.make_async_copy(
            rate_made.at[slot], rate_out.at[lines, step // shares], rate_out_sem.at[slot]
        )

    table_copy(0, 0).start()
    for turn in range(1, dip_count):
        rate_copy(turn).wait()

    @pl.loop(early, band // SUB)
    def _(block):
        send_back(block)

    for turn in range(dip_count):
        block = (dip + dip_count - turn) % dip_count
        lines = pl.ds(pl.multiple_of(block * cells_y, INNER), cells_y)
        value = rate_held[turn].T
        high = value.astype(jnp.bfloat16)
        joined[0, lines] = high
        joined[1, lines] = (value - high.astype(jnp.float32)).astype(jnp.bfloat16)

    @pl.loop(0, rate_steps)
    def _(step):
        slot = step % 2

        @pl.when(step + 1 < rate_steps)
        def _():
            table_copy(step + 1, 1 - slot).start()

        table_copy(step, slot).wait()

        @pl.when(step >= 2)
        def _():
            rate_out_copy(step - 2, slot).wait()

        dot = functools.partial(jnp.dot, preferred_element_type=jnp.float32)
        first, second = table_held[slot, 0], table_held[slot, 1]
        value = dot(first, joined[0]) + (dot(first, joined[1]) + dot(second, joined[0]))
        rate_made[slot] = value.reshape(taken, 2, band, rows)
        rate_out_copy(step, slot).start()

    for step in range(rate_steps - 2, rate_steps):
        rate_out_copy(step, step % 2).wait()

    @pl.loop(0, band // SUB)
    def _(block):
        back_own_copy(block).wait()

        @pl.loop(1, group)
        def _(offset):
            back_copy(offset, block).wait()


def stress_back(strike_count, dip_count, slip, rate, kernel, history, tables, turns, twists):
    half = dip_count // 2
    cells_x, cells_y = slip.shape
    lags, band, total_x = kernel.shape
    total_y = cells_y * dip_count
    rows = cells_x // half
    group = strike_count * half
    outer = total_x // INNER
    chunk = cells_x // CHUNKS
    depth = 2 * SUB
    parts = max(4, CHUNKS * depth // band)
    taken = 2
    lines = strike_count * 2 * band
    assert INNER == 2 * outer and band % depth == 0 and chunk % INNER == 0
    f32, b16, dma = jnp.float32, jnp.bfloat16, pltpu.SemaphoreType.DMA
    whole = pl.BlockSpec(memory_space=pl.ANY)
    size = band * total_x
    return pl.pallas_call(
        functools.partial(stress_kernel, strike_count, dip_count),
        out_shape=[
            jax.ShapeDtypeStruct((group, 2, band, rows), f32),
            jax.ShapeDtypeStruct((strike_count, half, 2, band, rows), f32),
        ],
        in_specs=[whole] * 6 + [pl.BlockSpec(memory_space=pltpu.VMEM)] * 2,
        out_specs=[whole] * 2,
        scratch_shapes=[
            pltpu.VMEM((half, cells_x, cells_y), f32),
            pltpu.VMEM((strike_count, 2, band, cells_x), f32),
            pltpu.VMEM((strike_count, 2, band, cells_x), f32),
            pltpu.VMEM((group, 2, band, rows), f32),
            pltpu.VMEM((2, lines, half * cells_y), b16),
            pltpu.VMEM((2, strike_count * 2, half * cells_y), b16),
            pltpu.VMEM((strike_count * 2, cells_x // INNER, INNER), f32),
            pltpu.VMEM((strike_count * 2, cells_x // INNER, INNER), f32),
            pltpu.VMEM((strike_count, 2, cells_x // INNER, INNER), f32),
            pltpu.VMEM((2, lags, depth, total_x // parts), b16),
            pltpu.VMEM((2, lags, 2, depth, total_x // parts), b16),
            pltpu.VMEM((2, band, total_x), f32),
            pltpu.VMEM((outer * SUB, 2 * INNER), f32),
            pltpu.VMEM((2, strike_count, outer // strike_count, SUB, INNER), f32),
            pltpu.VMEM((2, outer * SUB, INNER), f32),
            pltpu.VMEM((2, outer * SUB, INNER), f32),
            pltpu.VMEM((dip_count, rows, cells_y), f32),
            pltpu.VMEM((2, total_y, rows), b16),
            pltpu.VMEM((2, 2, taken * 2 * band, total_y), b16),
            pltpu.VMEM((2, taken, 2, band, rows), f32),
            dma((4,)),
            dma((2,)),
            dma((2,)),
            dma((2, 2)),
            dma((2, max(1, half - 1), CHUNKS)),
            dma((2,)),
            dma((2, strike_count - 1)),
            dma((2, strike_count - 1, CHUNKS)),
            dma((CHUNKS,)),
            dma((2, dip_count - 1)),
            dma((2, group - 1, band // SUB)),
            dma((band // SUB,)),
        ],
        compiler_params=pltpu.CompilerParams(
            vmem_limit_bytes=56 * 1024 * 1024, collective_id=0, has_side_effects=True
        ),
        cost_estimate=pl.CostEstimate(
            flops=size * 8000, bytes_accessed=size * 120, transcendentals=size
        ),
    )(slip, rate, kernel, history, *tables, turns, twists)


def line_kernel(where_in, back, table, out):
    half = back.shape[1]
    total = None
    for place in range(half):
        value = back[:, place].reshape(-1, back.shape[3])
        high = value.astype(jnp.bfloat16)
        low = (value - high.astype(jnp.float32)).astype(jnp.bfloat16)

        def dot(left, right):
            return lax.dot_general(
                left, right, (((0,), (0,)), ((), ())), preferred_element_type=jnp.float32
            )

        first, second = table[0, 0, place], table[0, 1, place]
        value = dot(high, first) + (dot(low, first) + dot(high, second))
        total = value if total is None else total + value
    out[...] = total


def line_piece(where, back, table, cells_y):
    _, _, half, lines, total_y = table.shape
    strike_count, _, both, rows = back.shape
    return pl.pallas_call(
        line_kernel,
        out_shape=jax.ShapeDtypeStruct((rows, cells_y), jnp.float32),
        grid_spec=pltpu.PrefetchScalarGridSpec(
            num_scalar_prefetch=1,
            grid=(1,),
            in_specs=[
                pl.BlockSpec(back.shape, lambda step, where: (0, 0, 0, 0)),
                pl.BlockSpec(
                    (1, 2, half, lines, cells_y),
                    lambda step, where: (where[0], 0, 0, 0, where[3]),
                ),
            ],
            out_specs=pl.BlockSpec((rows, cells_y), lambda step, where: (0, 0)),
        ),
        compiler_params=pltpu.CompilerParams(vmem_limit_bytes=48 * 1024 * 1024),
        cost_estimate=pl.CostEstimate(
            flops=6 * half * lines * rows * cells_y,
            bytes_accessed=8 * half * lines * rows,
            transcendentals=0,
        ),
    )(where, back, table)


def modes_kernel(strike_count, piece_in, turns_in, twists_in, out, spectrum, grid, natural, mixed):
    outer = twists_in.shape[2]
    tiles = outer // strike_count
    share = piece_in.shape[3] // INNER
    groups = piece_in.shape[2] // SUB
    for group in range(groups):
        lines = slice(group * SUB, (group + 1) * SUB)

        def load(source, part):
            places = [(source * tiles + tile) // share for tile in range(tiles)]
            offsets = [(source * tiles + tile) % share * INNER for tile in range(tiles)]
            return jnp.stack(
                [
                    piece_in[place, part, lines, offset : offset + INNER]
                    for place, offset in zip(places, offsets)
                ]
            )

        forward(load, turns_in, twists_in, spectrum, grid, strike_count)
        for part in range(2):
            natural[part] = spectrum[:, part * INNER : (part + 1) * INNER]
            reorder(natural.at[part], mixed.at[group, part], outer)
    for part in range(2):
        for at in range(outer):
            lines = slice(at * SUB, (at + 1) * SUB)
            tile = jnp.concatenate([mixed[group, part, lines, :] for group in range(groups)], 0)
            out[part, :, at * INNER : (at + 1) * INNER] = tile.astype(jnp.bfloat16)


def modes(strike_count, piece, turns, twists):
    sources, _, band, chunk = piece.shape
    total = sources * chunk
    outer = total // INNER
    lines = 2 * SUB
    assert INNER == 2 * outer and band % lines == 0
    size = band * total
    return pl.pallas_call(
        functools.partial(modes_kernel, strike_count),
        grid=(band // lines,),
        out_shape=jax.ShapeDtypeStruct((2, band, total), jnp.bfloat16),
        in_specs=[
            pl.BlockSpec((sources, 2, lines, chunk), lambda step: (0, 0, step, 0)),
            pl.BlockSpec(turns.shape, lambda step: (0,) * 4),
            pl.BlockSpec(twists.shape, lambda step: (0,) * 5),
        ],
        out_specs=pl.BlockSpec((2, lines, total), lambda step: (0, step, 0)),
        scratch_shapes=[
            pltpu.VMEM((outer * SUB, 2 * INNER), jnp.float32),
            pltpu.VMEM((2, strike_count, outer // strike_count, SUB, INNER), jnp.float32),
            pltpu.VMEM((2, outer * SUB, INNER), jnp.float32),
            pltpu.VMEM((2, 2, outer * SUB, INNER), jnp.float32),
        ],
        compiler_params=pltpu.CompilerParams(vmem_limit_bytes=32 * 1024 * 1024),
        cost_estimate=pl.CostEstimate(
            flops=size * 2000, bytes_accessed=size * 12, transcendentals=0
        ),
    )(piece, turns, twists)


def tie_kernel(value, earlier, out):
    del value, earlier, out


def tie(value, earlier):
    whole = pl.BlockSpec(memory_space=pl.ANY)
    return pl.pallas_call(
        tie_kernel,
        out_shape=jax.ShapeDtypeStruct(value.shape, value.dtype),
        in_specs=[whole] * 2,
        out_specs=whole,
        input_output_aliases={0: 0},
    )(value, earlier)


def per_device(
    slip,
    slip_rate,
    state,
    loading,
    normal_stress,
    patch,
    rate_coef,
    state_coef,
    slip_scale,
    kernel,
    history,
):
    strike_count = lax.axis_size("strike")
    dip_count = lax.axis_size("dip")
    half = dip_count // 2
    both_axes = ("strike", "dip")
    cells_x, cells_y = slip.shape
    band, total_x = kernel.shape[1:]
    total_y = cells_y * dip_count
    rows = cells_x // half
    strike, dip = lax.axis_index("strike"), lax.axis_index("dip")
    side, place = dip // half, dip % half
    sides = [
        [s * dip_count + t * half + k for s in range(strike_count) for k in range(half)]
        for t in range(2)
    ]

    def across_half(array):
        return lax.all_to_all(
            array, both_axes, split_axis=0, concat_axis=0, tiled=True, axis_index_groups=sides
        )

    def turn_dip(array, turn):
        return lax.ppermute(array, "dip", [(d, (d + turn) % dip_count) for d in range(dip_count)])

    turns, twists = (jnp.asarray(value) for value in strike_tables(total_x, strike_count))
    tables = [jnp.asarray(value) for value in dip_tables(strike_count, dip_count, band, total_y)]
    back, rate_parts = stress_back(
        strike_count, dip_count, slip, slip_rate, kernel, history, tables, turns, twists
    )
    back = back.reshape(strike_count, half, 2 * band, rows)
    cells = (slip_rate, state, loading, normal_stress, patch)

    def where(turn):
        return jnp.stack([side, dip, place, (dip + turn) % dip_count])

    rate_both = across_half(rate_parts.reshape(-1, 2, band, rows))
    pieces = {}
    for turn in sorted(range(dip_count), key=lambda turn: (turn == 0, turn % half, turn < half)):
        piece = line_piece(where(turn), back, tables[0], cells_y)
        if turn % half:
            piece = tie(piece, rate_both)
        pieces[turn] = turn_dip(piece, turn) if turn else piece
    rate_modes = modes(strike_count, rate_both, turns, twists)
    outs = []
    for turn in range(half):
        outs = friction(
            ((dip + dip_count - turn) % half).reshape(1),
            (rate_coef, state_coef, slip_scale),
            (pieces[turn], pieces[turn + half]),
            cells,
            [] if turn else [rate_modes],
            outs,
        )
    return (*outs, rate_modes)


def solution(mesh):
    return jax.shard_map(
        per_device,
        mesh=mesh,
        in_specs=(
            P("strike", "dip"),
            P("strike", "dip"),
            P("strike", "dip"),
            P("strike", "dip"),
            P("strike", "dip"),
            P("strike", "dip"),
            P(),
            P(),
            P(),
            P(None, ("strike", "dip"), None),
            P(None, None, ("strike", "dip"), None),
        ),
        out_specs=(
            P("strike", "dip"),
            P("strike", "dip"),
            P("strike", "dip"),
            P(None, ("strike", "dip"), None),
        ),
        check_vma=False,
    )
```

```python
import functools
import math

import jax
import jax.numpy as jnp
import numpy as np
from jax import lax
from jax.experimental import pallas as pl
from jax.experimental.pallas import tpu as pltpu
from jax.sharding import PartitionSpec as P

NEWTON = 8


shear_modulus = 1.0
damping = 0.5
relaxation = 0.35
time_step = 0.1


def inverse_sinh(value):
    size_v = jnp.abs(value)
    square = size_v * size_v
    result = jnp.log1p(size_v + square / (1.0 + jnp.sqrt(square + 1.0)))
    return jnp.where(value < 0.0, -result, result)


INNER = 128
SUB = 8
CHUNKS = 4
EARLY_PART = 2
MESH = pl.DeviceIdType.MESH


def wavenumber(index, count):
    return 2.0 * math.pi / count * ((index + count // 2) % count - count // 2).astype(jnp.float32)


def friction_kernel(
    labels,
    filled,
    where_in,
    rate_coef,
    state_coef,
    slip_scale,
    transfer_in,
    transfer_add,
    slip_rate_in,
    state_in,
    loading_in,
    normal_in,
    patch_in,
    *refs,
):
    new_rate_out, new_state_out, transfer_out = refs[filled:]
    patch = patch_in[...]

    def choose(table):
        result = jnp.zeros(patch.shape, jnp.float32)
        for label in range(labels):
            result = jnp.where(patch == label, table[label], result)
        return result

    coef_a = choose(rate_coef)
    coef_b = choose(state_coef)
    length_l = choose(slip_scale)
    transfer = transfer_in[...] + transfer_add[...]
    state = state_in[...]
    stress = loading_in[...] + transfer
    prefix = 2.0 * jnp.exp(-state / coef_a)
    angle_w = inverse_sinh(slip_rate_in[...] / prefix)
    weight = normal_in[...] * coef_a
    half = 0.5 * damping * prefix
    for iteration in range(NEWTON):
        raised = jnp.exp(angle_w)
        square = raised * raised
        residue = half * (square - 1.0) + (weight * angle_w - stress) * raised
        slope = half * (square + 1.0) + weight * raised
        angle_w = angle_w - relaxation * residue / (slope + jnp.abs(residue))
    new_rate = (0.5 * prefix) * (jnp.exp(angle_w) - jnp.exp(-angle_w))
    new_rate_out[...] = new_rate
    new_state_out[...] = state + time_step * (coef_b / length_l) * (
        jnp.exp(-state / coef_b) - jnp.abs(new_rate)
    )
    transfer_out[...] = transfer


def friction(where, tables, transfers, cells, earlier, before):
    rows, columns = transfers[0].shape
    blocks = 2
    step_rows = rows // blocks
    block = pl.BlockSpec((step_rows, columns), lambda step, where: (where[0] * blocks + step, 0))
    local = pl.BlockSpec((step_rows, columns), lambda step, where: (step, 0))
    scalar = pl.BlockSpec(memory_space=pltpu.SMEM)
    size = rows * columns
    first = 1 + len(tables) + 2 + len(cells) + len(earlier)
    kept = len(earlier) + len(before)
    return pl.pallas_call(
        functools.partial(friction_kernel, tables[0].shape[0], kept),
        out_shape=[jax.ShapeDtypeStruct(cells[0].shape, jnp.float32)] * 3,
        grid_spec=pltpu.PrefetchScalarGridSpec(
            num_scalar_prefetch=1,
            grid=(blocks,),
            in_specs=[scalar] * len(tables)
            + [local] * 2
            + [block] * len(cells)
            + [pl.BlockSpec(memory_space=pl.ANY)] * kept,
            out_specs=[block] * 3,
        ),
        input_output_aliases={first + index: index for index in range(len(before))},
        compiler_params=pltpu.CompilerParams(vmem_limit_bytes=32 * 1024 * 1024),
        cost_estimate=pl.CostEstimate(
            flops=size * 200, bytes_accessed=size * 40, transcendentals=size * 30
        ),
    )(where, *tables, *transfers, *cells, *earlier, *before)


def split_parts(value):
    high = value.astype(jnp.bfloat16)
    return np.stack([high, (value - high.astype(np.float32)).astype(jnp.bfloat16)])


def dip_tables(strike_count, dip_count, band, total):
    half = dip_count // 2
    index = np.arange(total).reshape(strike_count, 2, half, band).transpose(1, 2, 0, 3)
    turn = index[..., None] * np.arange(total) % total * (2.0 * np.pi / total)
    table = np.stack([np.cos(turn), -np.sin(turn)], 3) / math.sqrt(total)
    mirrored = table[:, 0, :, :, 0].reshape(2, strike_count * 2, total)
    table = table.reshape(2, half, strike_count * 2 * band, total)
    return [
        np.ascontiguousarray(np.moveaxis(split_parts(part.astype(np.float32)), 0, 1))
        for part in (table, mirrored)
    ]


def lane_order(outer):
    fold = INNER // outer
    return (np.arange(outer)[None, :] * fold + np.arange(fold)[:, None]).reshape(-1)


def strike_tables(total, sources):
    outer = total // INNER
    order = lane_order(outer)
    turn = np.arange(INNER)[:, None] * order[None, :] % INNER * (2.0 * np.pi / INNER)
    cos, sin = np.cos(turn) / math.sqrt(total), np.sin(turn) / math.sqrt(total)
    there = np.block([[cos, -sin], [sin, cos]])
    back = np.block([[cos.T, sin.T], [-sin.T, cos.T]])
    both = np.stack([there, back]).astype(np.float32)
    high = both.astype(jnp.bfloat16)
    low = (both - high.astype(np.float32)).astype(jnp.bfloat16)
    twist = np.arange(outer)[:, None] * np.arange(INNER)[None, :] * (2.0 * np.pi / total)
    twist = np.stack([np.cos(twist), np.sin(twist)])
    tiles = outer // sources
    small = np.arange(sources)[:, None] * np.arange(tiles)[None, :] * (2.0 * np.pi / outer)
    small = np.stack([np.cos(small), np.sin(small)]).reshape(2, outer)
    twists = np.stack([twist, np.broadcast_to(small[:, :, None], twist.shape)])
    twists = np.broadcast_to(twists[:, :, :, None, :], (2, 2, outer, SUB, INNER))
    return np.stack([high, low], 1), np.ascontiguousarray(twists.astype(np.float32))


def times_root(value, step, count, sign):
    re, im = value
    if step == 0:
        return re, im
    if 4 * step == count:
        return (-im, re) if sign > 0 else (im, -re)
    if 8 * step == count or 8 * step == 3 * count:
        root = math.sqrt(0.5)
        if sign > 0:
            turned = (re - im, re + im) if 8 * step == count else (-re - im, re - im)
        else:
            turned = (re + im, im - re) if 8 * step == count else (im - re, -re - im)
        return turned[0] * root, turned[1] * root
    cos = math.cos(2.0 * math.pi * step / count)
    sin = sign * math.sin(2.0 * math.pi * step / count)
    return re * cos - im * sin, re * sin + im * cos


def short_transform(values, sign):
    count = len(values)
    if count == 1:
        return values
    even = short_transform(values[0::2], sign)
    odd = short_transform(values[1::2], sign)
    low, high = [], []
    for step in range(count // 2):
        turned = times_root(odd[step], step, count, sign)
        low.append((even[step][0] + turned[0], even[step][1] + turned[1]))
        high.append((even[step][0] - turned[0], even[step][1] - turned[1]))
    return low + high


def exact_dot(left, table):
    high = left.astype(jnp.bfloat16)
    low = (left - high.astype(jnp.float32)).astype(jnp.bfloat16)
    dot = functools.partial(jnp.dot, preferred_element_type=jnp.float32)
    return dot(high, table[0]) + (dot(low, table[0]) + dot(high, table[1]))


def forward(load, turns_in, twists_in, spectrum, grid, sources):
    outer = twists_in.shape[2]
    tiles = outer // sources
    values = [(load(source, 0), load(source, 1)) for source in range(sources)]
    for at, (re, im) in enumerate(short_transform(values, -1.0)):
        lines = slice(at * tiles, (at + 1) * tiles)
        cos, sin = twists_in[1, 0, lines], twists_in[1, 1, lines]
        grid[0, at] = re * cos + im * sin
        grid[1, at] = im * cos - re * sin
    values = [(grid[0, :, tile], grid[1, :, tile]) for tile in range(tiles)]
    for at, (re, im) in enumerate(short_transform(values, -1.0)):
        lines = slice(at * sources, (at + 1) * sources)
        cos, sin = twists_in[0, 0, lines], twists_in[0, 1, lines]
        lines = slice(at * sources * SUB, (at + 1) * sources * SUB)
        spectrum[lines, :INNER] = (re * cos + im * sin).reshape(-1, INNER)
        spectrum[lines, INNER:] = (im * cos - re * sin).reshape(-1, INNER)
    spectrum[...] = exact_dot(spectrum[...], turns_in[0])


def backward(store, turns_in, twists_in, spectrum, grid, sources):
    outer = twists_in.shape[2]
    tiles = outer // sources
    spectrum[...] = exact_dot(spectrum[...], turns_in[1])
    values = []
    for at in range(tiles):
        lines = slice(at * sources * SUB, (at + 1) * sources * SUB)
        re = spectrum[lines, :INNER].reshape(sources, SUB, INNER)
        im = spectrum[lines, INNER:].reshape(sources, SUB, INNER)
        lines = slice(at * sources, (at + 1) * sources)
        cos, sin = twists_in[0, 0, lines], twists_in[0, 1, lines]
        values.append((re * cos - im * sin, re * sin + im * cos))
    for tile, (re, im) in enumerate(short_transform(values, 1.0)):
        grid[0, :, tile] = re
        grid[1, :, tile] = im
    values = []
    for at in range(sources):
        lines = slice(at * tiles, (at + 1) * tiles)
        cos, sin = twists_in[1, 0, lines], twists_in[1, 1, lines]
        re, im = grid[0, at], grid[1, at]
        values.append((re * cos - im * sin, re * sin + im * cos))
    for source, pair in enumerate(short_transform(values, 1.0)):
        for part in range(2):
            store(source, part, pair[part])


def reorder(source, target, outer):
    lane = lax.broadcasted_iota(jnp.int32, (outer, INNER), 1)
    for row in range(0, SUB, 2):
        pair = [source[pl.ds(row + at, outer, stride=SUB), :] for at in range(2)]
        turned = jnp.concatenate(pair, 0).T
        upper, lower = turned[:outer], turned[outer:]
        first = jnp.where(lane < outer, upper, pltpu.roll(lower, outer, 1))
        second = jnp.where(lane < outer, pltpu.roll(upper, outer, 1), lower)
        target[pl.ds(row, outer, stride=SUB), :] = first
        target[pl.ds(row + 1, outer, stride=SUB), :] = second


def dot_rows(table, value):
    high = value.astype(jnp.bfloat16)
    low = (value - high.astype(jnp.float32)).astype(jnp.bfloat16)

    def dot(left, right):
        return lax.dot_general(
            left, right, (((1,), (1,)), ((), ())), preferred_element_type=jnp.float32
        )

    return dot(table[0], high) + (dot(table[0], low) + dot(table[1], high))


def stress_kernel(
    strike_count,
    dip_count,
    slip,
    rate,
    kernel,
    history,
    table_all,
    mirror_all,
    turns_in,
    twists_in,
    back_out,
    rate_out,
    slip_held,
    made,
    held,
    sent,
    table,
    mirror,
    extra_made,
    extra_held,
    extra_parts,
    kernel_held,
    history_held,
    memory,
    spectrum,
    grid,
    natural,
    mixed,
    rate_held,
    joined,
    table_held,
    rate_made,
    local_sem,
    table_sem,
    rate_out_sem,
    memory_sem,
    slip_sem,
    extra_sem,
    extra_part_sem,
    band_sem,
    own_sem,
    rate_sem,
    back_sem,
    back_own_sem,
):
    half = dip_count // 2
    strike, dip = lax.axis_index("strike"), lax.axis_index("dip")
    side, place = dip // half, dip % half
    cells_x, cells_y = slip.shape
    lags, _, band, total_x = history.shape
    total_y = cells_y * dip_count
    rows = cells_x // half
    group = strike_count * half
    me = strike * half + place
    chunk = cells_x // CHUNKS
    outer = total_x // INNER
    tiles = outer // strike_count

    def in_half(index):
        return (index // half, side * half + index % half)

    barrier = pltpu.get_barrier_semaphore()

    @pl.loop(1, group)
    def _(offset):
        pl.semaphore_signal(
            barrier, inc=1, device_id=in_half((me + offset) % group), device_id_type=MESH
        )

    for other in range(half):
        pl.semaphore_signal(
            barrier,
            inc=1,
            device_id=(strike, (1 - side) * half + other),
            device_id_type=MESH,
        )
    pl.semaphore_wait(barrier, group - 1 + half)

    def slip_copy(offset, part):
        lines = pl.ds(part * chunk, chunk)
        return pltpu.make_async_remote_copy(
            src_ref=slip.at[lines],
            dst_ref=slip_held.at[place, lines],
            send_sem=slip_sem.at[0, offset - 1, part],
            recv_sem=slip_sem.at[1, offset - 1, part],
            device_id=(strike, side * half + (place + offset) % half),
            device_id_type=MESH,
        )

    for part in range(CHUNKS):
        for offset in range(1, half):
            slip_copy(offset, part).start()
    columns = pl.ds(pl.multiple_of(side * half * cells_y, INNER), half * cells_y)
    firsts = [
        pltpu.make_async_copy(slip, slip_held.at[place], local_sem.at[0]),
        pltpu.make_async_copy(table_all.at[side, :, place, :, columns], table, local_sem.at[1]),
        pltpu.make_async_copy(mirror_all.at[1 - side, :, :, columns], mirror, local_sem.at[2]),
        pltpu.make_async_copy(
            rate.at[pl.ds(pl.multiple_of(place * rows, SUB), rows)], rate_held.at[0], local_sem.at[3]
        ),
    ]
    for copy in firsts:
        copy.start()

    depth, width = kernel_held.shape[2:]
    across = total_x // width
    steps = band // depth * across

    def memory_copies(step, slot):
        lines = pl.ds(pl.multiple_of(step // across * depth, depth), depth)
        lanes = pl.ds(pl.multiple_of(step % across * width, width), width)
        return (
            pltpu.make_async_copy(
                kernel.at[:, lines, lanes], kernel_held.at[slot], memory_sem.at[0, slot]
            ),
            pltpu.make_async_copy(
                history.at[:, :, lines, lanes], history_held.at[slot], memory_sem.at[1, slot]
            ),
        )

    for copy in memory_copies(0, 0):
        copy.start()

    def memory_step(step):
        slot = step % 2

        @pl.when(step + 1 < steps)
        def _():
            for copy in memory_copies(step + 1, 1 - slot):
                copy.start()

        for copy in memory_copies(step, slot):
            copy.wait()
        piece = 2 * INNER

        @pl.loop(0, width // piece)
        def _(at):
            lanes = pl.ds(pl.multiple_of(at * piece, piece), piece)
            sums = [jnp.zeros((depth, piece), jnp.float32) for _ in range(2)]
            for lag in range(lags):
                factor = kernel_held[slot, lag, :, lanes].astype(jnp.float32)
                for part in range(2):
                    past = history_held[slot, lag, part, :, lanes].astype(jnp.float32)
                    sums[part] = sums[part] + factor * past
            lines = pl.ds(pl.multiple_of(step // across * depth, depth), depth)
            lanes = pl.ds(pl.multiple_of(step % across * width + at * piece, piece), piece)
            for part in range(2):
                memory[part, lines, lanes] = sums[part]

    def rate_copy(turn):
        target = (dip + turn) % dip_count
        lines = pl.ds(pl.multiple_of(target % half * rows, SUB), rows)
        return pltpu.make_async_remote_copy(
            src_ref=rate.at[lines],
            dst_ref=rate_held.at[turn],
            send_sem=rate_sem.at[0, turn - 1],
            recv_sem=rate_sem.at[1, turn - 1],
            device_id=(strike, target),
            device_id_type=MESH,
        )

    def extra_copy():
        return pltpu.make_async_remote_copy(
            src_ref=extra_made,
            dst_ref=extra_held,
            send_sem=extra_sem.at[0],
            recv_sem=extra_sem.at[1],
            device_id=(strike, (dip + half) % dip_count),
            device_id_type=MESH,
        )

    def extra_part_copy(offset):
        target = (strike + offset) % strike_count
        return pltpu.make_async_remote_copy(
            src_ref=extra_held.at[pl.ds(2 * target, 2)],
            dst_ref=extra_parts.at[strike],
            send_sem=extra_part_sem.at[0, offset - 1],
            recv_sem=extra_part_sem.at[1, offset - 1],
            device_id=(target, dip),
            device_id_type=MESH,
        )

    def band_copy(offset, part):
        lanes = pl.ds(pl.multiple_of(part * chunk, INNER), chunk)
        target = (strike + offset) % strike_count
        return pltpu.make_async_remote_copy(
            src_ref=made.at[target, :, :, lanes],
            dst_ref=held.at[strike, :, :, lanes],
            send_sem=band_sem.at[0, offset - 1, part],
            recv_sem=band_sem.at[1, offset - 1, part],
            device_id=(target, dip),
            device_id_type=MESH,
        )

    def own_copy(part):
        lanes = pl.ds(pl.multiple_of(part * chunk, INNER), chunk)
        return pltpu.make_async_copy(
            made.at[strike, :, :, lanes], held.at[strike, :, :, lanes], own_sem.at[part]
        )

    def start_rate(turn, early):
        middle = ((dip == half - 1) & (turn == 1)) | ((dip == half) & (turn == dip_count - 1))

        @pl.when(middle == early)
        def _():
            rate_copy(turn).start()

    for turn in range(1, dip_count):
        start_rate(turn, True)
    for copy in firsts:
        copy.wait()

    @pl.loop(0, CHUNKS)
    def _(part):
        @pl.loop(0, steps // CHUNKS)
        def _(step):
            memory_step(part * (steps // CHUNKS) + step)

        for offset in range(1, half):
            slip_copy(offset, part).wait()

        @pl.when(part == CHUNKS - 2)
        def _():
            for turn in range(1, dip_count):
                start_rate(turn, False)

        lines = pl.ds(pl.multiple_of(part * chunk, SUB), chunk)
        lanes = pl.ds(pl.multiple_of(part * chunk, INNER), chunk)
        blocks = [slip_held[block, lines] for block in range(half)]
        extra = sum(
            dot_rows(mirror[:, :, block * cells_y : (block + 1) * cells_y], blocks[block])
            for block in range(half)
        )
        for tile in range(chunk // INNER):
            for at in range(2 * strike_count):
                extra_made[at, pl.ds(part * (chunk // INNER) + tile, 1), :] = extra[
                    at : at + 1, tile * INNER : (tile + 1) * INNER
                ]
        value = sum(
            dot_rows(table[:, :, block * cells_y : (block + 1) * cells_y], blocks[block])
            for block in range(half)
        )
        made[:, :, :, lanes] = value.reshape(strike_count, 2, band, chunk)

        own_copy(part).start()

        @pl.loop(1, strike_count)
        def _(offset):
            band_copy(offset, part).start()

    extra_copy().start()
    extra_copy().wait()

    @pl.loop(1, strike_count)
    def _(offset):
        extra_part_copy(offset).start()

    own_extra = pltpu.make_async_copy(
        extra_held.at[pl.ds(2 * strike, 2)], extra_parts.at[strike], local_sem.at[0]
    )
    own_extra.start()

    @pl.loop(0, CHUNKS)
    def _(part):
        own_copy(part).wait()

        @pl.loop(1, strike_count)
        def _(offset):
            band_copy(offset, part).wait()

    own_extra.wait()

    @pl.loop(1, strike_count)
    def _(offset):
        extra_part_copy(offset).wait()

    keep = jnp.where(place == 0, 1.0, 0.0)

    @pl.loop(0, strike_count)
    def _(source):
        for side_part in range(2):
            for tile in range(tiles):
                lanes = slice(tile * INNER, (tile + 1) * INNER)
                held[source, side_part, 0:1, lanes] = (
                    held[source, side_part, 0:1, lanes]
                    + keep * extra_parts[source, side_part, tile : tile + 1, :]
                )

    def back_copy(offset, block):
        lines = pl.ds(pl.multiple_of(block * SUB, SUB), SUB)
        target = (me + offset) % group
        return pltpu.make_async_remote_copy(
            src_ref=sent.at[target, :, lines],
            dst_ref=back_out.at[me, :, lines],
            send_sem=back_sem.at[0, offset - 1, block],
            recv_sem=back_sem.at[1, offset - 1, block],
            device_id=in_half(target),
            device_id_type=MESH,
        )

    def back_own_copy(block):
        lines = pl.ds(pl.multiple_of(block * SUB, SUB), SUB)
        return pltpu.make_async_copy(
            sent.at[me, :, lines], back_out.at[me, :, lines], back_own_sem.at[block]
        )

    def send_back(block):
        back_own_copy(block).start()

        @pl.loop(1, group)
        def _(offset):
            back_copy(offset, block).start()

    early = band // SUB // EARLY_PART

    @pl.loop(0, band // SUB)
    def _(block):
        lines = pl.ds(pl.multiple_of(block * SUB, SUB), SUB)

        def load(source, part):
            return jnp.stack(
                [
                    held[source, part, lines, tile * INNER : (tile + 1) * INNER]
                    for tile in range(tiles)
                ]
            )

        forward(load, turns_in, twists_in, spectrum, grid, strike_count)
        for part in range(2):
            for at in range(outer):
                natural[part, at * SUB : (at + 1) * SUB, :] = memory[
                    part, lines, at * INNER : (at + 1) * INNER
                ]
            reorder(natural.at[part], mixed.at[part], outer)
        shape = (outer * SUB, INNER)
        line = lax.broadcasted_iota(jnp.int32, shape, 0)
        lane = lax.broadcasted_iota(jnp.int32, shape, 1)
        mode_x = line // SUB + lane // outer * outer + lane % outer * INNER
        row = line % SUB + block * SUB
        wave_x = wavenumber(mode_x, total_x)
        wave_y = wavenumber((strike * dip_count + dip) * band + row, total_y)
        times = jnp.where((row == 0) & (place == 0), 1.0, 2.0)
        static = (-0.5 * shear_modulus) * times * jnp.sqrt(wave_y * wave_y + wave_x * wave_x)
        spectrum[:, :INNER] = static * spectrum[:, :INNER] + mixed[0]
        spectrum[:, INNER:] = static * spectrum[:, INNER:] + mixed[1]
        share = tiles // half

        def store(source, part, value):
            for tile in range(tiles):
                lanes = slice(tile % share * INNER, (tile % share + 1) * INNER)
                sent[source * half + tile // share, part, lines, lanes] = value[tile]

        backward(store, turns_in, twists_in, spectrum, grid, strike_count)
        @pl.when(block < early)
        def _():
            send_back(block)

    taken = table_held.shape[2] // (2 * band)
    shares = strike_count // taken
    rate_steps = half * shares

    def table_copy(step, slot):
        lines = pl.ds(pl.multiple_of(step % shares * taken * 2 * band, 2 * SUB), taken * 2 * band)
        return pltpu.make_async_copy(
            table_all.at[side, :, step // shares, lines], table_held.at[slot], table_sem.at[slot]
        )

    def rate_out_copy(step, slot):
        lines = pl.ds(step % shares * taken, taken)
        return pltpu.make_async_copy(
            rate_made.at[slot], rate_out.at[lines, step // shares], rate_out_sem.at[slot]
        )

    table_copy(0, 0).start()
    for turn in range(1, dip_count):
        rate_copy(turn).wait()

    @pl.loop(early, band // SUB)
    def _(block):
        send_back(block)

    for turn in range(dip_count):
        block = (dip + dip_count - turn) % dip_count
        lines = pl.ds(pl.multiple_of(block * cells_y, INNER), cells_y)
        value = rate_held[turn].T
        high = value.astype(jnp.bfloat16)
        joined[0, lines] = high
        joined[1, lines] = (value - high.astype(jnp.float32)).astype(jnp.bfloat16)

    @pl.loop(0, rate_steps)
    def _(step):
        slot = step % 2

        @pl.when(step + 1 < rate_steps)
        def _():
            table_copy(step + 1, 1 - slot).start()

        table_copy(step, slot).wait()

        @pl.when(step >= 2)
        def _():
            rate_out_copy(step - 2, slot).wait()

        dot = functools.partial(jnp.dot, preferred_element_type=jnp.float32)
        first, second = table_held[slot, 0], table_held[slot, 1]
        value = dot(first, joined[0]) + (dot(first, joined[1]) + dot(second, joined[0]))
        rate_made[slot] = value.reshape(taken, 2, band, rows)
        rate_out_copy(step, slot).start()

    for step in range(rate_steps - 2, rate_steps):
        rate_out_copy(step, step % 2).wait()

    @pl.loop(0, band // SUB)
    def _(block):
        back_own_copy(block).wait()

        @pl.loop(1, group)
        def _(offset):
            back_copy(offset, block).wait()


def stress_back(strike_count, dip_count, slip, rate, kernel, history, tables, turns, twists):
    half = dip_count // 2
    cells_x, cells_y = slip.shape
    lags, band, total_x = kernel.shape
    total_y = cells_y * dip_count
    rows = cells_x // half
    group = strike_count * half
    outer = total_x // INNER
    chunk = cells_x // CHUNKS
    depth = 2 * SUB
    parts = max(4, CHUNKS * depth // band)
    taken = 2
    lines = strike_count * 2 * band
    assert INNER == 2 * outer and band % depth == 0 and chunk % INNER == 0
    f32, b16, dma = jnp.float32, jnp.bfloat16, pltpu.SemaphoreType.DMA
    whole = pl.BlockSpec(memory_space=pl.ANY)
    size = band * total_x
    return pl.pallas_call(
        functools.partial(stress_kernel, strike_count, dip_count),
        out_shape=[
            jax.ShapeDtypeStruct((group, 2, band, rows), f32),
            jax.ShapeDtypeStruct((strike_count, half, 2, band, rows), f32),
        ],
        in_specs=[whole] * 6 + [pl.BlockSpec(memory_space=pltpu.VMEM)] * 2,
        out_specs=[whole] * 2,
        scratch_shapes=[
            pltpu.VMEM((half, cells_x, cells_y), f32),
            pltpu.VMEM((strike_count, 2, band, cells_x), f32),
            pltpu.VMEM((strike_count, 2, band, cells_x), f32),
            pltpu.VMEM((group, 2, band, rows), f32),
            pltpu.VMEM((2, lines, half * cells_y), b16),
            pltpu.VMEM((2, strike_count * 2, half * cells_y), b16),
            pltpu.VMEM((strike_count * 2, cells_x // INNER, INNER), f32),
            pltpu.VMEM((strike_count * 2, cells_x // INNER, INNER), f32),
            pltpu.VMEM((strike_count, 2, cells_x // INNER, INNER), f32),
            pltpu.VMEM((2, lags, depth, total_x // parts), b16),
            pltpu.VMEM((2, lags, 2, depth, total_x // parts), b16),
            pltpu.VMEM((2, band, total_x), f32),
            pltpu.VMEM((outer * SUB, 2 * INNER), f32),
            pltpu.VMEM((2, strike_count, outer // strike_count, SUB, INNER), f32),
            pltpu.VMEM((2, outer * SUB, INNER), f32),
            pltpu.VMEM((2, outer * SUB, INNER), f32),
            pltpu.VMEM((dip_count, rows, cells_y), f32),
            pltpu.VMEM((2, total_y, rows), b16),
            pltpu.VMEM((2, 2, taken * 2 * band, total_y), b16),
            pltpu.VMEM((2, taken, 2, band, rows), f32),
            dma((4,)),
            dma((2,)),
            dma((2,)),
            dma((2, 2)),
            dma((2, max(1, half - 1), CHUNKS)),
            dma((2,)),
            dma((2, strike_count - 1)),
            dma((2, strike_count - 1, CHUNKS)),
            dma((CHUNKS,)),
            dma((2, dip_count - 1)),
            dma((2, group - 1, band // SUB)),
            dma((band // SUB,)),
        ],
        compiler_params=pltpu.CompilerParams(
            vmem_limit_bytes=56 * 1024 * 1024, collective_id=0, has_side_effects=True
        ),
        cost_estimate=pl.CostEstimate(
            flops=size * 8000, bytes_accessed=size * 120, transcendentals=size
        ),
    )(slip, rate, kernel, history, *tables, turns, twists)


def line_kernel(where_in, back, table, out):
    half = back.shape[1]
    total = None
    for place in range(half):
        value = back[:, place].reshape(-1, back.shape[3])
        high = value.astype(jnp.bfloat16)
        low = (value - high.astype(jnp.float32)).astype(jnp.bfloat16)

        def dot(left, right):
            return lax.dot_general(
                left, right, (((0,), (0,)), ((), ())), preferred_element_type=jnp.float32
            )

        first, second = table[0, 0, place], table[0, 1, place]
        value = dot(high, first) + (dot(low, first) + dot(high, second))
        total = value if total is None else total + value
    out[...] = total


def line_piece(where, back, table, cells_y):
    _, _, half, lines, total_y = table.shape
    strike_count, _, both, rows = back.shape
    return pl.pallas_call(
        line_kernel,
        out_shape=jax.ShapeDtypeStruct((rows, cells_y), jnp.float32),
        grid_spec=pltpu.PrefetchScalarGridSpec(
            num_scalar_prefetch=1,
            grid=(1,),
            in_specs=[
                pl.BlockSpec(back.shape, lambda step, where: (0, 0, 0, 0)),
                pl.BlockSpec(
                    (1, 2, half, lines, cells_y),
                    lambda step, where: (where[0], 0, 0, 0, where[3]),
                ),
            ],
            out_specs=pl.BlockSpec((rows, cells_y), lambda step, where: (0, 0)),
        ),
        compiler_params=pltpu.CompilerParams(vmem_limit_bytes=48 * 1024 * 1024),
        cost_estimate=pl.CostEstimate(
            flops=6 * half * lines * rows * cells_y,
            bytes_accessed=8 * half * lines * rows,
            transcendentals=0,
        ),
    )(where, back, table)


def modes_kernel(strike_count, piece_in, turns_in, twists_in, out, spectrum, grid, natural, mixed):
    outer = twists_in.shape[2]
    tiles = outer // strike_count
    share = piece_in.shape[3] // INNER
    groups = piece_in.shape[2] // SUB
    for group in range(groups):
        lines = slice(group * SUB, (group + 1) * SUB)

        def load(source, part):
            places = [(source * tiles + tile) // share for tile in range(tiles)]
            offsets = [(source * tiles + tile) % share * INNER for tile in range(tiles)]
            return jnp.stack(
                [
                    piece_in[place, part, lines, offset : offset + INNER]
                    for place, offset in zip(places, offsets)
                ]
            )

        forward(load, turns_in, twists_in, spectrum, grid, strike_count)
        for part in range(2):
            natural[part] = spectrum[:, part * INNER : (part + 1) * INNER]
            reorder(natural.at[part], mixed.at[group, part], outer)
    for part in range(2):
        for at in range(outer):
            lines = slice(at * SUB, (at + 1) * SUB)
            tile = jnp.concatenate([mixed[group, part, lines, :] for group in range(groups)], 0)
            out[part, :, at * INNER : (at + 1) * INNER] = tile.astype(jnp.bfloat16)


def modes(strike_count, piece, turns, twists):
    sources, _, band, chunk = piece.shape
    total = sources * chunk
    outer = total // INNER
    lines = 2 * SUB
    assert INNER == 2 * outer and band % lines == 0
    size = band * total
    return pl.pallas_call(
        functools.partial(modes_kernel, strike_count),
        grid=(band // lines,),
        out_shape=jax.ShapeDtypeStruct((2, band, total), jnp.bfloat16),
        in_specs=[
            pl.BlockSpec((sources, 2, lines, chunk), lambda step: (0, 0, step, 0)),
            pl.BlockSpec(turns.shape, lambda step: (0,) * 4),
            pl.BlockSpec(twists.shape, lambda step: (0,) * 5),
        ],
        out_specs=pl.BlockSpec((2, lines, total), lambda step: (0, step, 0)),
        scratch_shapes=[
            pltpu.VMEM((outer * SUB, 2 * INNER), jnp.float32),
            pltpu.VMEM((2, strike_count, outer // strike_count, SUB, INNER), jnp.float32),
            pltpu.VMEM((2, outer * SUB, INNER), jnp.float32),
            pltpu.VMEM((2, 2, outer * SUB, INNER), jnp.float32),
        ],
        compiler_params=pltpu.CompilerParams(vmem_limit_bytes=32 * 1024 * 1024),
        cost_estimate=pl.CostEstimate(
            flops=size * 2000, bytes_accessed=size * 12, transcendentals=0
        ),
    )(piece, turns, twists)


def tie_kernel(value, earlier, out):
    del value, earlier, out


def tie(value, earlier):
    whole = pl.BlockSpec(memory_space=pl.ANY)
    return pl.pallas_call(
        tie_kernel,
        out_shape=jax.ShapeDtypeStruct(value.shape, value.dtype),
        in_specs=[whole] * 2,
        out_specs=whole,
        input_output_aliases={0: 0},
    )(value, earlier)


def per_device(
    slip,
    slip_rate,
    state,
    loading,
    normal_stress,
    patch,
    rate_coef,
    state_coef,
    slip_scale,
    kernel,
    history,
):
    strike_count = lax.axis_size("strike")
    dip_count = lax.axis_size("dip")
    half = dip_count // 2
    both_axes = ("strike", "dip")
    cells_x, cells_y = slip.shape
    band, total_x = kernel.shape[1:]
    total_y = cells_y * dip_count
    rows = cells_x // half
    strike, dip = lax.axis_index("strike"), lax.axis_index("dip")
    side, place = dip // half, dip % half
    sides = [
        [s * dip_count + t * half + k for s in range(strike_count) for k in range(half)]
        for t in range(2)
    ]

    def across_half(array):
        return lax.all_to_all(
            array, both_axes, split_axis=0, concat_axis=0, tiled=True, axis_index_groups=sides
        )

    def turn_dip(array, turn):
        return lax.ppermute(array, "dip", [(d, (d + turn) % dip_count) for d in range(dip_count)])

    turns, twists = (jnp.asarray(value) for value in strike_tables(total_x, strike_count))
    tables = [jnp.asarray(value) for value in dip_tables(strike_count, dip_count, band, total_y)]
    back, rate_parts = stress_back(
        strike_count, dip_count, slip, slip_rate, kernel, history, tables, turns, twists
    )
    back = back.reshape(strike_count, half, 2 * band, rows)
    cells = (slip_rate, state, loading, normal_stress, patch)

    def where(turn):
        return jnp.stack([side, dip, place, (dip + turn) % dip_count])

    rate_both = across_half(rate_parts.reshape(-1, 2, band, rows))
    pieces = {}
    for turn in sorted(range(dip_count), key=lambda turn: (turn == 0, turn % half, turn < half)):
        piece = line_piece(where(turn), back, tables[0], cells_y)
        if turn % half:
            piece = tie(piece, rate_both)
        pieces[turn] = turn_dip(piece, turn) if turn else piece
    rate_modes = modes(strike_count, rate_both, turns, twists)
    outs = []
    for turn in range(half):
        outs = friction(
            ((dip + dip_count - turn) % half).reshape(1),
            (rate_coef, state_coef, slip_scale),
            (pieces[turn], pieces[turn + half]),
            cells,
            [] if turn else [rate_modes],
            outs,
        )
    return (*outs, rate_modes)


def solution(mesh):
    return jax.shard_map(
        per_device,
        mesh=mesh,
        in_specs=(
            P("strike", "dip"),
            P("strike", "dip"),
            P("strike", "dip"),
            P("strike", "dip"),
            P("strike", "dip"),
            P("strike", "dip"),
            P(),
            P(),
            P(),
            P(None, ("strike", "dip"), None),
            P(None, None, ("strike", "dip"), None),
        ),
        out_specs=(
            P("strike", "dip"),
            P("strike", "dip"),
            P("strike", "dip"),
            P(None, ("strike", "dip"), None),
        ),
        check_vma=False,
    )
```
